32 devices in a mesh: groups: 2 (over x), ctx: 16 (over z, y, core).
Axes of the slice: x: 2, y: 2, z: 4, core: 2. Of those that a mesh axis runs over, the one named last changes fastest.
Arguments:
- query_rows: float32 [8192, 768], P(('groups', 'ctx')), parts along dimension 0, may hold values from -6 to 6
- key_rows: float32 [8192, 768], P(('groups', 'ctx')), parts along dimension 0, may hold values from -6 to 6
- value_rows: float32 [8192, 768], P(('groups', 'ctx')), parts along dimension 0, may hold values from -6 to 6
- grad_rows: float32 [8192, 768], P(('groups', 'ctx')), parts along dimension 0, may hold values from -6 to 6
- placement: int32 [128], P(('groups', 'ctx')), parts along dimension 0, may hold values from 0 to 63, as said below
- cell_lengths: int32 [128], P(('groups', 'ctx')), parts along dimension 0, may hold values from 16 to 64
- gene_mask: int32 [128, 3], P(('groups', 'ctx')), parts along dimension 0, may hold values 0 or 1
Outputs:
- grad_queries: float32 [8192, 768], P(('groups', 'ctx')), parts along dimension 0
- grad_keys: float32 [8192, 768], P(('groups', 'ctx')), parts along dimension 0
- grad_values: float32 [8192, 768], P(('groups', 'ctx')), parts along dimension 0
The draws below stay inside these ranges and needn't reach their ends.
There are 2 independent parts, one for each index of `groups`. The reference program is written for one: setup_inputs(seed, part) draws one part's arguments, and reference() takes and returns one part's arrays. A program takes and returns all parts, laid end to end along the dimension named above; each array names one. Nothing has to cross between parts.
Inputs may be any that keep to these rules, and one draw needn't show every extreme that they name: `placement`: A permutation of the slots. The cells of ctx index d (cells d * 4 to d * 4 + 3) take slots of block d or of block (d + 1) mod 16; exactly 2 of them take slots of the next block.
All inputs are finite; a program needn't handle non-finite values. No bound on the sum of `gene_mask` on one device may be relied on, other than what follows from the above.
Results may differ from the reference program's by a relative error of at most 0.0003.
Values sent between devices are 32-bit elements; how exact they have to be, the bound alone decides.
No kernel may reach another device: no remote copies, remote signals or barrier semaphores. Data moves between devices by JAX's collectives and lax.ppermute only.
A program may use at most 64 MiB of HBM per device.

```python
import jax
import jax.numpy as jnp
from jax import lax

HEAD_DIM = 64
D = 768
CELL_LEN = 64
GBLOCK = 16
CELL_DEV = 4
MOVE = 2
WINDOW = 4
CELLS = 64
TOKENS = 4096
GMASKS = 3
N_CTX = 16


def drawn_rows(key):
    return jnp.clip(jax.random.normal(key, (TOKENS, D)), -6.0, 6.0)


def draw_query_rows(key, part):
    sampled = drawn_rows(jax.random.fold_in(key, 1)).reshape(CELLS, CELL_LEN, D)
    return sampled.reshape(TOKENS, D)


def draw_key_rows(key, part):
    sampled = drawn_rows(jax.random.fold_in(key, 2)).reshape(CELLS, CELL_LEN, D)
    return sampled.reshape(TOKENS, D)


def draw_placement(key, part):
    devices = CELLS // CELL_DEV
    first_key, second_key = jax.random.split(key)
    ranking = jax.vmap(lambda subkey: jax.random.permutation(subkey, CELL_DEV))(jax.random.split(first_key, devices))
    ordering = jnp.argsort(ranking, axis=1)
    starts = (jnp.arange(devices) * CELL_DEV)[:, None]
    leaving = jnp.roll(ordering[:, :MOVE] + starts, 1, axis=0)
    staying = ordering[:, MOVE:] + starts
    arriving = jnp.concatenate([leaving, staying], axis=1)
    slot_ids = jax.vmap(lambda subkey: jax.random.permutation(subkey, CELL_DEV))(jax.random.split(second_key, devices)) + starts
    return jnp.zeros((CELLS,), jnp.int32).at[arriving.reshape(-1)].set(slot_ids.reshape(-1).astype(jnp.int32))


def place_ends(entries, stream_key, least, top_value):
    spot = [jax.random.randint(jax.random.fold_in(stream_key, axis), (), 0, length) for axis, length in enumerate(entries.shape)]
    longest = entries.shape.index(max(entries.shape))
    beside = spot[:longest] + [(spot[longest] + 1) % entries.shape[longest]] + spot[longest + 1:]
    return entries.at[tuple(spot)].set(least).at[tuple(beside)].set(top_value)


def shard_levels(rng, dims, shards, smallest, largest):
    loudness = 1.0
    for dim, parts in shards:
        steps = jax.random.uniform(jax.random.fold_in(jax.random.fold_in(rng, 6), dim), (parts,), jnp.float32, smallest / len(shards), largest / len(shards))
        loudness = loudness * jnp.repeat(jnp.exp(steps), dims[dim] // parts).reshape((-1,) + (1,) * (len(dims) - 1 - dim))
    return loudness


def centred(own_key, shape, width, reach, cuts=(), kind=jnp.bfloat16):
    entries = jax.random.normal(own_key, shape, jnp.float32) * width
    if len(cuts) > 0:
        entries = shard_levels(own_key, shape, cuts, -0.22, 0.18) * entries
    return jnp.clip(entries, min=-reach, max=reach).astype(kind)


def setup_inputs(seed: int = 0, part: int = 0) -> dict:
    streams_of = jax.random.split(jax.random.key(seed), 8)
    part_splits = jax.random.split(jax.random.fold_in(streams_of[7], part), 8)
    query_rows = draw_query_rows(jax.random.fold_in(jax.random.fold_in(streams_of[7], part), 71), part)
    key_rows = draw_key_rows(jax.random.fold_in(jax.random.fold_in(streams_of[7], part), 71), part)
    value_rows = centred(part_splits[2], (TOKENS, D), 1.0, 6.0, ((0, 16),), jnp.float32)
    grad_rows = centred(part_splits[3], (TOKENS, D), 1.0, 6.0, ((0, 16),), jnp.float32)
    placement = draw_placement(jax.random.fold_in(jax.random.fold_in(streams_of[7], part), 71), part)
    cell_lengths = place_ends(jax.random.randint(part_splits[5], (CELLS,), GBLOCK, CELL_LEN + 1), jax.random.fold_in(part_splits[5], 1), GBLOCK, CELL_LEN).astype(jnp.int32)
    gene_mask = place_ends((jax.random.randint(part_splits[6], (CELLS, GMASKS), 0, 3) < 1).astype(jnp.int32), jax.random.fold_in(part_splits[6], 1), 0, 1)
    return dict(query_rows=query_rows, key_rows=key_rows, value_rows=value_rows, grad_rows=grad_rows, placement=placement, cell_lengths=cell_lengths, gene_mask=gene_mask)


HIGH = lax.Precision.HIGHEST
NEGATIVE = -1.0e30


def token_flags(cell_lengths, gene_mask):
    position = jnp.arange(CELL_LEN)
    live_tokens = position[None, :] < cell_lengths[:, None]
    hidden_gene = jnp.concatenate([jnp.zeros((cell_lengths.shape[0], 1), jnp.int32), gene_mask.astype(jnp.int32)], axis=1)
    blocked = jnp.take(hidden_gene, position // GBLOCK, axis=1) > 0
    return live_tokens, jnp.logical_and(live_tokens, jnp.logical_not(blocked))


def reference(query_rows, key_rows, value_rows, grad_rows, placement, cell_lengths, gene_mask):
    devices = N_CTX
    row_count = CELL_DEV * CELL_LEN
    head_count = D // HEAD_DIM
    score_scale = HEAD_DIM ** -0.5
    live_tokens, key_ok = token_flags(cell_lengths, gene_mask)
    grad_live = grad_rows.reshape(CELLS, CELL_LEN, D) * live_tokens[:, :, None].astype(grad_rows.dtype)
    inverse = jnp.argsort(placement)

    def arrange(array):
        return array.reshape(CELLS, CELL_LEN, D)[inverse].reshape(devices, row_count, head_count, HEAD_DIM)

    query_all = arrange(query_rows)
    key_all = arrange(key_rows)
    value_all = arrange(value_rows)
    grad_all = arrange(grad_live)
    okay_all = key_ok[inverse].reshape(devices, row_count)
    offsets = jnp.arange(WINDOW)

    def one_device(running, position):
        key_sum, value_sum = running
        sources = (position - offsets) % devices
        key_block = key_all[sources].reshape(WINDOW * row_count, head_count, HEAD_DIM)
        value_block = value_all[sources].reshape(WINDOW * row_count, head_count, HEAD_DIM)
        okay_block = okay_all[sources].reshape(WINDOW * row_count)
        query_block = query_all[position]
        grad_block = grad_all[position]
        mask_row = okay_block[None, None, :]
        scores = jnp.einsum("qhd,khd->hqk", query_block, key_block, precision=HIGH) * score_scale
        masked = jnp.where(mask_row, scores, NEGATIVE)
        row_top = jnp.max(masked, axis=-1)
        total = jnp.sum(jnp.where(mask_row, jnp.exp(masked - row_top[:, :, None]), 0.0), axis=-1)
        log_total = row_top + jnp.log(total)
        weights = jnp.where(mask_row, jnp.exp(masked - log_total[:, :, None]), 0.0)
        output = jnp.einsum("hqk,khd->qhd", weights, value_block, precision=HIGH)
        row_delta = jnp.sum(grad_block * output, axis=-1).T
        grad_weights = jnp.einsum("qhd,khd->hqk", grad_block, value_block, precision=HIGH)
        grad_scores = weights * (grad_weights - row_delta[:, :, None])
        grad_query = jnp.einsum("hqk,khd->qhd", grad_scores, key_block, precision=HIGH) * score_scale
        grad_key = jnp.einsum("hqk,qhd->khd", grad_scores, query_block, precision=HIGH) * score_scale
        grad_value = jnp.einsum("hqk,qhd->khd", weights, grad_block, precision=HIGH)
        grad_key = grad_key.reshape(WINDOW, row_count, head_count, HEAD_DIM)
        grad_value = grad_value.reshape(WINDOW, row_count, head_count, HEAD_DIM)
        return (key_sum.at[sources].add(grad_key), value_sum.at[sources].add(grad_value)), grad_query

    empty_grads = jnp.zeros((devices, row_count, head_count, HEAD_DIM), jnp.float32)
    (key_sum, value_sum), query_sum = lax.scan(one_device, (empty_grads, empty_grads), jnp.arange(devices))

    def to_home(array):
        return array.reshape(CELLS, CELL_LEN, D)[placement].reshape(TOKENS, D)

    return to_home(query_sum), to_home(key_sum), to_home(value_sum)
```

```python
import functools

import jax
import jax.numpy as jnp
from jax import lax
from jax.experimental import pallas as pl
from jax.experimental.pallas import tpu as pltpu
from jax.sharding import PartitionSpec as P

HEAD_DIM = 64
CELL = 64
CELLS = 4
ROWS = 256
PLANE = 4
HEADS = 3
HALO = 14
F32 = jnp.float32
BF16 = jnp.bfloat16
VMEM = pltpu.VMEM
NEGATIVE = -1e30
SCALE = HEAD_DIM ** -0.5


def vspec():
    return pl.BlockSpec(memory_space=pltpu.VMEM)


def sspec():
    return pl.BlockSpec(memory_space=pltpu.SMEM)


def params(limit=32):
    return pltpu.CompilerParams(vmem_limit_bytes=limit << 20)


def cost(flops, nbytes):
    return pl.CostEstimate(flops=flops, bytes_accessed=nbytes, transcendentals=0)


def lanes(shape):
    return lax.broadcasted_iota(jnp.int32, shape, 1)


def swap_half(x):
    return pltpu.roll(x, 64, 1)


def join(low, high):
    return jnp.where(lanes(low.shape) < 64, low, high)


def cells(i):
    return pl.ds(pl.multiple_of(i * CELL, CELL), CELL)


def pack_kernel(first_of, with_meta, info, a_hbm, b_hbm, *refs):
    mine, core, ys = refs[0], refs[1], refs[2:8]
    a_ref, b_ref, sems = refs[8:]
    copies = []
    for i, (src, dst) in enumerate(((a_hbm, a_ref), (b_hbm, b_ref))):
        for c in range(CELLS):
            r = pl.ds(c * CELL, CELL)
            copies.append(pltpu.make_async_copy(src.at[r], dst.at[r], sems.at[i, c]))
            copies[-1].start()
    me = info[24]
    if with_meta:
        lane = lax.broadcasted_iota(jnp.int32, (8, 128), 1)
        meta = jnp.zeros((8, 128), F32)
        for i in range(20):
            meta = jnp.where(lane == i, info[i].astype(F32), meta)
        mine[pl.ds(HEADS * ROWS, 8), :] = meta
        core[pl.ds(HEADS * ROWS, 8), :] = meta
        ys[0][pl.ds(ROWS, 8), :] = meta
        ys[1][pl.ds(ROWS, 8), :] = meta
    row = lax.broadcasted_iota(jnp.int32, (CELL, 128), 0)
    for c in range(CELLS):
        copies[c].wait()
        copies[CELLS + c].wait()
        r = pl.ds(c * CELL, CELL)
        for s in range(PLANE):
            j = lax.bitwise_xor(me, s)
            first = pl.ds(pl.multiple_of(j * 128, 128), 128)
            last = pl.ds(pl.multiple_of((4 + j // 2) * 128, 128), 128)
            odd = (j % 2) == 1
            a, b = first_of(info, row, c, a_ref[r, first], b_ref[r, first])
            x, y = first_of(info, row, c, a_ref[r, last], b_ref[r, last])
            x = jnp.where(odd, swap_half(x), x)
            y = jnp.where(odd, y, swap_half(y))
            heads = (join(a, swap_half(b)), join(swap_half(a), b), join(x, y))
            for h in range(HEADS):
                if s == 0:
                    mine[pl.ds(h * ROWS + c * CELL, CELL), :] = heads[h]
                elif s == 1:
                    core[pl.ds(h * ROWS + c * CELL, CELL), :] = heads[h]
                else:
                    ys[2 * h + s - 2][pl.ds(c * CELL, CELL), :] = heads[h]


def plain(info, row, c, a, b):
    return a, b


def scaled(info, row, c, a, b):
    return a * SCALE, jnp.where(row < info[4 + c], b, 0.0)


def pack_heads(first_of, with_meta, info, a, b):
    extra = 8 if with_meta else 0
    shapes = [(HEADS * ROWS + extra, 128)] * 2 + [(ROWS + extra, 128)] * 2 + [(ROWS, 128)] * 4
    return pl.pallas_call(
        functools.partial(pack_kernel, first_of, with_meta),
        out_shape=[jax.ShapeDtypeStruct(s, F32) for s in shapes],
        in_specs=[sspec()] + [pl.BlockSpec(memory_space=pltpu.HBM)] * 2,
        out_specs=[vspec()] * 8,
        scratch_shapes=[
            VMEM(a.shape, F32),
            VMEM(b.shape, F32),
            pltpu.SemaphoreType.DMA((2, CELLS)),
        ],
        compiler_params=params(),
        cost_estimate=cost(1 << 20, 3 << 20),
        name="pack_heads",
    )(info, a, b)


def walk(meta, start, total, visit):
    rank = jnp.int32(0)
    for s in range(PLANE):
        for c in range(CELLS):
            rel = lax.rem(meta[s, c] - start + total, total)
            moved = rel >= 16
            slot = jnp.where(moved, 12 + rank, rel - 4)
            visit(s, c, rel, slot)
            rank = rank + moved.astype(jnp.int32)


def row_of(h):
    return (h * ROWS, h * ROWS, 0, 0)


META_ROWS = (HEADS * ROWS, HEADS * ROWS, ROWS, ROWS)


def halo_kernel(total, h, info, meta, *refs):
    kv, out = refs[:4], refs[4]

    def visit(s, c, rel, slot):
        @pl.when(rel >= 4)
        def _():
            out[cells(slot), :] = kv[s][pl.ds(row_of(h)[s] + c * CELL, CELL), :]

    walk(meta, info[25], total, visit)
    if h == 0:
        out[pl.ds(HALO * CELL, 8), :] = jnp.zeros((8, 128), F32)
        for s in range(PLANE):
            out[pl.ds(HALO * CELL + s, 1), :] = kv[s][pl.ds(META_ROWS[s], 1), :]


def halo_message(total, h, info, meta, kv):
    rows = HALO * CELL + (8 if h == 0 else 0)
    return pl.pallas_call(
        functools.partial(halo_kernel, total, h),
        out_shape=jax.ShapeDtypeStruct((rows, 128), F32),
        in_specs=[sspec()] * 2 + [vspec()] * 4,
        out_specs=vspec(),
        compiler_params=params(),
        cost_estimate=cost(1 << 10, 1 << 20),
        name="halo_message",
    )(info, meta, *kv)


def movers_kernel(total, h, info, meta, *refs):
    qg, out = refs[:4], refs[4]

    def visit(s, c, rel, slot):
        @pl.when(rel >= 16)
        def _():
            out[cells(slot - 12), :] = qg[s][pl.ds(row_of(h)[s] + c * CELL, CELL), :]

    walk(meta, info[25], total, visit)


def movers_message(total, h, info, meta, qg):
    return pl.pallas_call(
        functools.partial(movers_kernel, total, h),
        out_shape=jax.ShapeDtypeStruct((2 * CELL, 128), F32),
        in_specs=[sspec()] * 2 + [vspec()] * 4,
        out_specs=vspec(),
        compiler_params=params(),
        cost_estimate=cost(1 << 10, 1 << 18),
        name="movers_message",
    )(info, meta, *qg)


def split(x):
    high = x.astype(BF16).astype(F32)
    return high, x - high


def nt(a, b):
    return lax.dot_general(a, b, (((1,), (1,)), ((), ())), preferred_element_type=F32)


def nn(a, b):
    return lax.dot_general(a, b, (((1,), (0,)), ((), ())), preferred_element_type=F32)


def tn(a, b):
    return lax.dot_general(a, b, (((0,), (0,)), ((), ())), preferred_element_type=F32)


def attend_kernel(total, h, info, meta, meta_prev, *refs):
    kv, halo, qg, qgm = refs[:4], refs[4], refs[5:9], refs[9]
    dkv, dq, back = refs[10:13]
    kcat, vcat, acc_k, acc_v, qcat, gcat, qrhs, grhs, s_scr, d_scr, dq_scr = refs[13:]
    start = info[25]
    start_prev = info[26]
    lane = lax.broadcasted_iota(jnp.int32, (CELL, 128), 1)
    row = lax.broadcasted_iota(jnp.int32, (CELL, 128), 0)
    low = lane < 64

    def put_key(x, slot, m, s, c):
        hidden = row >= m[s, 4 + c]
        for i in range(3):
            inside = (row >= 16 * (i + 1)) & (row < 16 * (i + 2))
            hidden = hidden | (inside & (m[s, 8 + 3 * c + i] > 0))
        bias = jnp.where(hidden & (lane == 64), NEGATIVE, 0.0)
        high, rest = split(x)
        high_r, rest_r = swap_half(high), swap_half(rest)
        mid, least = split(rest)
        kcat[cells(slot), pl.ds(0, 128)] = jnp.where(low, high, rest_r).astype(BF16)
        kcat[cells(slot), pl.ds(128, 128)] = jnp.where(low, high, bias).astype(BF16)
        kcat[cells(slot), pl.ds(256, 128)] = jnp.where(low, mid, swap_half(least)).astype(BF16)
        kcat[cells(slot), pl.ds(384, 128)] = jnp.where(low, high, 0.0).astype(BF16)
        vcat[cells(slot), pl.ds(0, 128)] = jnp.where(low, high_r, rest).astype(BF16)
        vcat[cells(slot), pl.ds(128, 128)] = jnp.where(low, high_r, 0.0).astype(BF16)

    one = jnp.where(lane == 64, 1.0, 0.0)

    def put_query(x, slot):
        high, rest = split(x)
        high_r, rest_r = swap_half(high), swap_half(rest)
        qcat[cells(slot), pl.ds(0, 128)] = jnp.where(low, high, high_r).astype(BF16)
        qcat[cells(slot), pl.ds(128, 128)] = jnp.where(low, rest, one).astype(BF16)
        mid, least = split(rest)
        qcat[cells(slot), pl.ds(256, 128)] = jnp.where(low, mid, high_r).astype(BF16)
        qcat[cells(slot), pl.ds(384, 128)] = jnp.where(low, least, 0.0).astype(BF16)
        gcat[cells(slot), pl.ds(0, 128)] = jnp.where(low, high_r, high).astype(BF16)
        gcat[cells(slot), pl.ds(128, 128)] = jnp.where(low, rest_r, 0.0).astype(BF16)
        qrhs[cells(slot), :] = jnp.where(low, high, rest_r).astype(BF16)
        grhs[cells(slot), :] = jnp.where(low, rest_r, high).astype(BF16)

    def own(s, c, rel, slot):
        @pl.when(rel < 16)
        def _():
            put_key(kv[s][pl.ds(row_of(h)[s] + c * CELL, CELL), :], 12 + rel, meta, s, c)
            put_query(qg[s][pl.ds(row_of(h)[s] + c * CELL, CELL), :], rel)

    walk(meta, start, total, own)

    def before(s, c, rel, slot):
        @pl.when(rel >= 4)
        def _():
            put_key(halo[cells(slot), :], rel - 4, meta_prev, s, c)

        @pl.when(rel >= 16)
        def _():
            put_query(qgm[cells(slot - 12), :], rel - 16)

    walk(meta_prev, start_prev, total, before)
    acc_k[...] = jnp.zeros(acc_k.shape, F32)
    acc_v[...] = jnp.zeros(acc_v.shape, F32)

    def fold(x, op):
        out = x[0:8]
        for i in range(1, ROWS // 8):
            out = op(out, x[8 * i : 8 * i + 8])
        return out

    def block(b, carry):
        q_rows = pl.ds(pl.multiple_of(b * ROWS, ROWS), ROWS)

        def k_rows(c):
            return pl.ds(pl.multiple_of((b + c) * ROWS, ROWS), ROWS)

        top = None
        for c in range(4):
            scores = nt(kcat[k_rows(c), :], qcat[q_rows, :])
            s_scr[pl.ds(c * ROWS, ROWS), :] = scores
            part = fold(scores, jnp.maximum)
            top = part if top is None else jnp.maximum(top, part)
        top = jnp.max(top, axis=0, keepdims=True)
        size = jnp.zeros((8, ROWS), F32)
        dots = jnp.zeros((8, ROWS), F32)
        for c in range(4):
            weights = jnp.exp(s_scr[pl.ds(c * ROWS, ROWS), :] - top)
            grad_weights = nt(vcat[k_rows(c), :], gcat[q_rows, :])
            s_scr[pl.ds(c * ROWS, ROWS), :] = weights
            d_scr[pl.ds(c * ROWS, ROWS), :] = grad_weights
            size = size + fold(weights, jnp.add)
            dots = dots + fold(weights * grad_weights, jnp.add)
        inverse = 1.0 / jnp.sum(size, axis=0, keepdims=True)
        delta = jnp.sum(dots, axis=0, keepdims=True) * inverse
        dq_t = jnp.zeros((128, ROWS), F32)
        for c in range(4):
            weights = s_scr[pl.ds(c * ROWS, ROWS), :] * inverse
            grad_scores = weights * (d_scr[pl.ds(c * ROWS, ROWS), :] - delta)
            high = weights.astype(BF16)
            rest = (weights - high.astype(F32)).astype(BF16)
            acc_v[k_rows(c), :] += nn(high, grhs[q_rows, :]) + nn(rest, grhs[q_rows, :])
            high = grad_scores.astype(BF16)
            rest = (grad_scores - high.astype(F32)).astype(BF16)
            acc_k[k_rows(c), :] += nn(high, qrhs[q_rows, :]) + nn(rest, qrhs[q_rows, :])
            keys = kcat[k_rows(c), pl.ds(0, 128)]
            dq_t = dq_t + tn(keys, high) + tn(keys, rest)
        dq_t = (dq_t[0:64] + dq_t[64:128]) * SCALE
        dq_scr[q_rows, :] = jnp.concatenate([dq_t, dq_t], axis=0).T
        return carry

    lax.fori_loop(0, 4, block, 0)

    def grad_kv(slot):
        a = acc_k[cells(slot), :]
        b = acc_v[cells(slot), :]
        return jnp.where(low, a + swap_half(a), b + swap_half(b))

    def own_out(s, c, rel, slot):
        here = rel < 16
        x = grad_kv(jnp.where(here, 12 + rel, 0))
        dkv[pl.ds(s * ROWS + c * CELL, CELL), :] = jnp.where(here, x, 0.0)
        x = dq_scr[cells(jnp.where(here, rel, 0)), :]
        half = pl.ds(s * 128 + (c // 2) * CELL, CELL)
        if c % 2 == 0:
            dq[half, :] = x
        else:
            dq[half, :] = jnp.where(low, dq[half, :], x)

    walk(meta, start, total, own_out)
    pair = pl.ds(HALO * CELL, CELL)

    def before_out(s, c, rel, slot):
        @pl.when(rel >= 4)
        def _():
            back[cells(slot), :] = grad_kv(rel - 4)

        @pl.when(rel >= 16)
        def _():
            x = dq_scr[cells(rel - 16), :]
            first = slot == 12
            back[pair, :] = jnp.where(low == first, x, back[pair, :])

    walk(meta_prev, start_prev, total, before_out)


def attend(total, h, info, meta, meta_prev, kv, halo, qg, qgm):
    shapes = [(4 * ROWS, 128), (2 * ROWS, 128), (HALO * CELL + CELL, 128)]
    keys, queries = 28 * CELL, 16 * CELL
    return pl.pallas_call(
        functools.partial(attend_kernel, total, h),
        out_shape=[jax.ShapeDtypeStruct(s, F32) for s in shapes],
        in_specs=[sspec()] * 3 + [vspec()] * 10,
        out_specs=[vspec()] * 3,
        scratch_shapes=[
            VMEM((keys, 512), BF16),
            VMEM((keys, 256), BF16),
            VMEM((keys, 128), F32),
            VMEM((keys, 128), F32),
            VMEM((queries, 512), BF16),
            VMEM((queries, 256), BF16),
            VMEM((queries, 128), BF16),
            VMEM((queries, 128), BF16),
            VMEM((4 * ROWS, ROWS), F32),
            VMEM((4 * ROWS, ROWS), F32),
            VMEM((queries, 128), F32),
        ],
        compiler_params=params(24),
        cost_estimate=cost(8 << 30, 8 << 20),
        name="attend",
    )(info, meta, meta_prev, *kv, halo, *qg, qgm)


OUT = ROWS + ROWS // 2


def finish_kernel(total, info, meta, dkv, dq, back, *outs):
    low = lanes((CELL, 128)) < 64
    pair = back[pl.ds(HALO * CELL, CELL), :]
    for s in range(PLANE):
        outs[s][pl.ds(ROWS, 128), :] = dq[pl.ds(s * 128, 128), :]

    def visit(s, c, rel, slot):
        out = outs[s]
        sent = rel >= 4
        x = jnp.where(sent, back[cells(jnp.where(sent, slot, 0)), :], 0.0)
        out[pl.ds(c * CELL, CELL), :] = dkv[pl.ds(s * ROWS + c * CELL, CELL), :] + x

        @pl.when(rel >= 16)
        def _():
            straight = (slot - 12) == (c % 2)
            x = jnp.where(straight, pair, swap_half(pair))
            half = pl.ds(ROWS + (c // 2) * CELL, CELL)
            out[half, :] = jnp.where(low == (c % 2 == 0), x, out[half, :])

    walk(meta, info[25], total, visit)


def finish(total, info, meta, dkv, dq, back):
    shapes = [(OUT, 128)] * 4
    return pl.pallas_call(
        functools.partial(finish_kernel, total),
        out_shape=[jax.ShapeDtypeStruct(s, F32) for s in shapes],
        in_specs=[sspec()] * 2 + [vspec()] * 3,
        out_specs=[vspec()] * 4,
        compiler_params=params(),
        cost_estimate=cost(1 << 10, 2 << 20),
        name="finish",
    )(info, meta, dkv, dq, back)


def unpack_kernel(info, *refs):
    parts, (oq, ok, ov) = refs[:12], refs[12:]
    me = info[24]

    def grads(s, c, h):
        return parts[4 * h + s][pl.ds(c * CELL, CELL), :]

    def query(s, c, h):
        x = parts[4 * h + s][pl.ds(ROWS + (c // 2) * CELL, CELL), :]
        return x, swap_half(x)

    for s in range(PLANE):
        j = lax.bitwise_xor(me, s)
        first = pl.ds(pl.multiple_of(j * 128, 128), 128)
        for c in range(CELLS):
            r = pl.ds(c * CELL, CELL)
            a, b = grads(s, c, 0), grads(s, c, 1)
            ok[r, first] = join(a, swap_half(b))
            ov[r, first] = join(swap_half(a), b)
            x0, y0 = query(s, c, 0)
            x1, y1 = query(s, c, 1)
            oq[r, first] = join(x0, y1) if c % 2 == 0 else join(y0, x1)
    for s in (0, 2):
        j = lax.bitwise_xor(me, s)
        even = (j % 2) == 0
        last = pl.ds(pl.multiple_of((4 + j // 2) * 128, 128), 128)
        for c in range(CELLS):
            r = pl.ds(c * CELL, CELL)
            u, w = grads(s, c, 2), grads(s + 1, c, 2)
            a, b = jnp.where(even, u, w), jnp.where(even, w, u)
            ok[r, last] = join(a, swap_half(b))
            ov[r, last] = join(swap_half(a), b)
            u, w = query(s, c, 2)[0], query(s + 1, c, 2)[0]
            a, b = jnp.where(even, u, w), jnp.where(even, w, u)
            oq[r, last] = join(a, swap_half(b)) if c % 2 == 0 else join(swap_half(a), b)


def unpack_heads(info, parts, features):
    return pl.pallas_call(
        unpack_kernel,
        out_shape=[jax.ShapeDtypeStruct((ROWS, features), F32)] * 3,
        in_specs=[sspec()] + [vspec()] * 12,
        out_specs=[vspec()] * 3,
        compiler_params=params(),
        cost_estimate=cost(1 << 20, 5 << 20),
        name="unpack_heads",
    )(info, *[x for part in parts for x in part])


def after(x, *earlier):
    return lax.optimization_barrier((x, *earlier))[0]


def on_device(query_rows, key_rows, value_rows, grad_rows, placement, cell_lengths, gene_mask):
    count = lax.axis_size("ctx")
    total = count * CELLS
    index = lax.axis_index("ctx").astype(jnp.int32)
    plane = index // PLANE

    def along_z(x, step):
        return lax.ppermute(x, "ctx", [(i, (i + step * PLANE) % count) for i in range(count)])

    def swap(x, bit):
        return lax.ppermute(x, "ctx", [(i, i ^ bit) for i in range(count)])

    start = plane * (PLANE * CELLS)
    start_prev = lax.rem(start - PLANE * CELLS + total, total)
    tail = jnp.stack([jnp.int32(0)] * 4 + [index % PLANE, start, start_prev, jnp.int32(0)])
    info = jnp.concatenate([placement, cell_lengths, gene_mask.reshape(-1), tail])

    kv_mine, kv_core, *kv_y = pack_heads(plain, True, info, key_rows, value_rows)

    def across(parts, h, *earlier):
        return [swap(after(parts[2 * h + i], *earlier), 2 + i) for i in range(2)]

    kv0 = across(kv_y, 0)
    kv_core = swap(kv_core, 1)
    qg_mine, qg_core, *qg_y = pack_heads(scaled, False, after(info, kv_mine), query_rows, grad_rows)
    qg0 = across(qg_y, 0)
    kv0 = list(after(tuple(kv0), qg_mine))
    kv1 = across(kv_y, 1, *kv0)
    kv = [(kv_mine, kv_core, *kv0)]
    meta = jnp.stack([x[r, :32] for x, r in zip(kv[0], META_ROWS)]).astype(jnp.int32)
    halo = [along_z(halo_message(total, 0, info, meta, kv[0]), 1)]
    qg_core = swap(after(qg_core, kv_core), 1)
    qg = [(qg_mine, qg_core, *qg0)]
    qgm = [along_z(movers_message(total, 0, info, meta, qg[0]), 1)]
    kv2 = across(kv_y, 2, *qg0)
    kv.append((kv_mine, kv_core, *kv1))
    halo.append(along_z(halo_message(total, 1, info, meta, kv[1]), 1))
    qg1 = across(qg_y, 1, *kv1)
    kv.append((kv_mine, kv_core, *kv2))
    halo.append(along_z(halo_message(total, 2, info, meta, kv[2]), 1))
    qg2 = across(qg_y, 2, *kv2)
    for y in (qg1, qg2):
        qg.append((qg_mine, qg_core, *y))
        qgm.append(along_z(movers_message(total, len(qg) - 1, info, meta, qg[-1]), 1))
    meta_prev = halo[0][HALO * CELL : HALO * CELL + 4, :32].astype(jnp.int32)

    parts = []
    turn = ()
    for h in range(HEADS):
        late = after(qgm[h], *turn)
        dkv, dq, back = attend(total, h, info, meta, meta_prev, kv[h], halo[h], qg[h], late)
        turn = (dq,)
        mine, *outs = finish(total, info, meta, dkv, dq, along_z(back, -1))
        parts.append([mine] + [swap(x, i + 1) for i, x in enumerate(outs)])
    return tuple(unpack_heads(info, parts, query_rows.shape[1]))


def solution(mesh):
    rows = P(("groups", "ctx"), None)
    flat = P(("groups", "ctx"))
    return jax.shard_map(
        on_device,
        mesh=mesh,
        in_specs=(rows, rows, rows, rows, flat, flat, rows),
        out_specs=(rows, rows, rows),
        check_vma=False,
    )
```

```python
import functools

import jax
import jax.numpy as jnp
from jax import lax
from jax.experimental import pallas as pl
from jax.experimental.pallas import tpu as pltpu
from jax.sharding import PartitionSpec as P

HEAD_DIM = 64
CELL = 64
CELLS = 4
ROWS = 256
PLANE = 4
HEADS = 3
HALO = 14
F32 = jnp.float32
BF16 = jnp.bfloat16
VMEM = pltpu.VMEM
NEGATIVE = -1e30
SCALE = HEAD_DIM ** -0.5


def vspec():
    return pl.BlockSpec(memory_space=pltpu.VMEM)


def sspec():
    return pl.BlockSpec(memory_space=pltpu.SMEM)


def params(limit=32):
    return pltpu.CompilerParams(vmem_limit_bytes=limit << 20)


def cost(flops, nbytes):
    return pl.CostEstimate(flops=flops, bytes_accessed=nbytes, transcendentals=0)


def lanes(shape):
    return lax.broadcasted_iota(jnp.int32, shape, 1)


def swap_half(x):
    return pltpu.roll(x, 64, 1)


def join(low, high):
    return jnp.where(lanes(low.shape) < 64, low, high)


def cells(i):
    return pl.ds(pl.multiple_of(i * CELL, CELL), CELL)


def head_blocks(info, c, s, a_ref, b_ref, grads):
    r = pl.ds(c * CELL, CELL)
    j = lax.bitwise_xor(info[24], s)
    first = pl.ds(pl.multiple_of(j * 128, 128), 128)
    last = pl.ds(pl.multiple_of((4 + j // 2) * 128, 128), 128)
    odd = (j % 2) == 1

    def load(lane_tile):
        a, b = a_ref[r, lane_tile], b_ref[r, lane_tile]
        if grads:
            row = lax.broadcasted_iota(jnp.int32, (CELL, 128), 0)
            a, b = a * SCALE, jnp.where(row < info[4 + c], b, 0.0)
        return a, b

    def zero():
        a, b = load(first)
        return join(a, swap_half(b))

    def one():
        a, b = load(first)
        return join(swap_half(a), b)

    def two():
        a, b = load(last)
        return join(jnp.where(odd, swap_half(a), a), jnp.where(odd, b, swap_half(b)))

    return zero, one, two


def pack_first_kernel(info, k_ref, v_ref, *outs):
    lane = lax.broadcasted_iota(jnp.int32, (8, 128), 1)
    meta = jnp.zeros((8, 128), F32)
    for i in range(20):
        meta = jnp.where(lane == i, info[i].astype(F32), meta)
    for s in range(PLANE):
        outs[s][pl.ds(ROWS, 8), :] = meta
        for c in range(CELLS):
            blocks = head_blocks(info, c, s, k_ref, v_ref, False)
            outs[s][pl.ds(c * CELL, CELL), :] = blocks[0]()


def pack_rest_kernel(info, k_ref, v_ref, q_ref, g_ref, *outs):
    mine, core, near, far = outs[0], outs[1], outs[2:5], outs[5:8]
    for s in range(PLANE):
        for c in range(CELLS):
            kv = head_blocks(info, c, s, k_ref, v_ref, False)
            qg = head_blocks(info, c, s, q_ref, g_ref, True)
            for i, block in enumerate((kv[1], kv[2], qg[0], qg[1], qg[2])):
                if s < 2:
                    outs[s][pl.ds(i * ROWS + c * CELL, CELL), :] = block()
                else:
                    part, row0 = ((1, 0), (2, 0), (0, 0), (1, ROWS), (2, ROWS))[i]
                    (near, far)[s - 2][part][pl.ds(row0 + c * CELL, CELL), :] = block()


def pack(kernel, shapes, name, info, *arrays):
    return pl.pallas_call(
        kernel,
        out_shape=[jax.ShapeDtypeStruct(s, F32) for s in shapes],
        in_specs=[sspec()] + [vspec()] * len(arrays),
        out_specs=[vspec()] * len(shapes),
        compiler_params=params(),
        cost_estimate=cost(1 << 20, 3 << 20),
        name=name,
    )(info, *arrays)


def walk(meta, start, total, visit):
    rank = jnp.int32(0)
    for s in range(PLANE):
        for c in range(CELLS):
            rel = lax.rem(meta[s, c] - start + total, total)
            moved = rel >= 16
            slot = jnp.where(moved, 12 + rank, rel - 4)
            visit(s, c, rel, slot)
            rank = rank + moved.astype(jnp.int32)


def halo_kernel(total, kv_rows, qg_rows, with_meta, info, meta, *refs):
    kv, qg, out = refs[:4], refs[4:-1], refs[-1]
    queries = 0 if kv_rows is None else HALO

    def visit(s, c, rel, slot):
        if kv_rows is not None:

            @pl.when(rel >= 4)
            def _():
                out[cells(slot), :] = kv[s][pl.ds(kv_rows[s] + c * CELL, CELL), :]

        if qg_rows is not None:

            @pl.when(rel >= 16)
            def _():
                out[cells(queries + slot - 12), :] = qg[s][pl.ds(qg_rows[s] + c * CELL, CELL), :]

    walk(meta, info[25], total, visit)
    if with_meta:
        out[pl.ds(HALO * CELL, 8), :] = jnp.zeros((8, 128), F32)
        for s in range(PLANE):
            out[pl.ds(HALO * CELL + s, 1), :] = kv[s][pl.ds(ROWS, 1), :]


def halo_message(total, info, meta, kv, qg, with_meta=False):
    rows, arrays = 0, []
    if kv is not None:
        rows += HALO * CELL
        arrays += [x for x, _ in kv]
    else:
        arrays += [x for x, _ in qg]
    if qg is not None:
        rows += 2 * CELL
        arrays += [x for x, _ in qg]
    rows += 8 if with_meta else 0
    firsts = [None if x is None else [r for _, r in x] for x in (kv, qg)]
    return pl.pallas_call(
        functools.partial(halo_kernel, total, *firsts, with_meta),
        out_shape=jax.ShapeDtypeStruct((rows, 128), F32),
        in_specs=[sspec()] * 2 + [vspec()] * len(arrays),
        out_specs=vspec(),
        compiler_params=params(),
        cost_estimate=cost(1 << 10, 1 << 20),
        name="halo_message",
    )(info, meta, *arrays)


def split(x):
    high = x.astype(BF16).astype(F32)
    return high, x - high


def nt(a, b):
    return lax.dot_general(a, b, (((1,), (1,)), ((), ())), preferred_element_type=F32)


def nn(a, b):
    return lax.dot_general(a, b, (((1,), (0,)), ((), ())), preferred_element_type=F32)


def tn(a, b):
    return lax.dot_general(a, b, (((0,), (0,)), ((), ())), preferred_element_type=F32)


def attend_kernel(total, kv_rows, qg_rows, m_row, info, meta, meta_prev, *refs):
    kv, halo, qg, qgm = refs[:4], refs[4], refs[5:9], refs[9]
    dkv, dq, back = refs[10:13]
    kcat, vcat, kt, acc_k, acc_v, qcat, gcat, qrhs, grhs, dq_scr = refs[13:23]
    pairs = (refs[23:25], refs[25:27])
    start = info[25]
    start_prev = info[26]
    lane = lax.broadcasted_iota(jnp.int32, (CELL, 128), 1)
    low = lane < 64
    lane16 = lax.broadcasted_iota(jnp.int32, (16, 128), 1)
    row16 = lax.broadcasted_iota(jnp.int32, (16, 128), 0)

    def put_key(x, slot, m, s, c):
        length = m[s, 4 + c]
        parts = []
        for i in range(4):
            limit = length - 16 * i
            if i > 0:
                limit = jnp.where(m[s, 7 + 3 * c + i] > 0, 0, limit)
            parts.append(jnp.where((row16 >= limit) & (lane16 == 64), NEGATIVE, 0.0))
        bias = jnp.concatenate(parts, axis=0)
        high, rest = split(x)
        high_r, rest_r = swap_half(high), swap_half(rest)
        mid, least = split(rest)
        kcat[cells(slot), pl.ds(0, 128)] = jnp.where(low, high, rest_r).astype(BF16)
        kcat[cells(slot), pl.ds(128, 128)] = jnp.where(low, high, bias).astype(BF16)
        kcat[cells(slot), pl.ds(256, 128)] = jnp.where(low, mid, swap_half(least)).astype(BF16)
        kcat[cells(slot), pl.ds(384, 128)] = jnp.where(low, high, 0.0).astype(BF16)
        vcat[cells(slot), pl.ds(0, 128)] = jnp.where(low, high_r, rest).astype(BF16)
        vcat[cells(slot), pl.ds(128, 128)] = jnp.where(low, high_r, 0.0).astype(BF16)

    one = jnp.where(lane == 64, 1.0, 0.0)

    def put_query(x, slot):
        high, rest = split(x)
        high_r, rest_r = swap_half(high), swap_half(rest)
        qcat[cells(slot), pl.ds(0, 128)] = jnp.where(low, high, high_r).astype(BF16)
        qcat[cells(slot), pl.ds(128, 128)] = jnp.where(low, rest, one).astype(BF16)
        mid, least = split(rest)
        qcat[cells(slot), pl.ds(256, 128)] = jnp.where(low, mid, high_r).astype(BF16)
        qcat[cells(slot), pl.ds(384, 128)] = jnp.where(low, least, 0.0).astype(BF16)
        gcat[cells(slot), pl.ds(0, 128)] = jnp.where(low, high_r, high).astype(BF16)
        gcat[cells(slot), pl.ds(128, 128)] = jnp.where(low, rest_r, 0.0).astype(BF16)
        qrhs[cells(slot), :] = jnp.where(low, high, rest_r).astype(BF16)
        grhs[cells(slot), :] = jnp.where(low, rest_r, high).astype(BF16)

    def own(s, c, rel, slot):
        here = rel < 16
        put_key(kv[s][pl.ds(kv_rows[s] + c * CELL, CELL), :], jnp.where(here, 12 + rel, 28), meta, s, c)
        put_query(qg[s][pl.ds(qg_rows[s] + c * CELL, CELL), :], jnp.where(here, rel, 16))

    walk(meta, start, total, own)
    came = [jnp.int32(0), jnp.int32(0)]

    def before(s, c, rel, slot):
        here = rel >= 4
        x = halo[cells(jnp.where(here, slot, 0)), :]
        put_key(x, jnp.where(here, rel - 4, 28), meta_prev, s, c)
        for i in range(2):
            came[i] = jnp.where((rel >= 16) & (slot == 12 + i), rel - 16, came[i])

    walk(meta_prev, start_prev, total, before)
    for i in range(2):
        put_query(qgm[pl.ds(m_row + i * CELL, CELL), :], came[i])
    for j in range(7):
        kt[:, pl.ds(j * ROWS, ROWS)] = kcat[pl.ds(j * ROWS, ROWS), pl.ds(0, 128)].T
    acc_k[...] = jnp.zeros(acc_k.shape, F32)
    acc_v[...] = jnp.zeros(acc_v.shape, F32)

    def fold(x, op):
        out = x[0:8]
        for i in range(1, x.shape[0] // 8):
            out = op(out, x[8 * i : 8 * i + 8])
        return out

    def block(b, carry):
        s_scr, d_scr = pairs[b % 2 if isinstance(b, int) else 0]

        def rows(i, n=ROWS):
            return pl.ds(i * ROWS if isinstance(i, int) else pl.multiple_of(i * ROWS, ROWS), n)

        q_rows = rows(b)
        top = None
        for c in range(4):
            scores = nt(kcat[rows(b + c), :], qcat[q_rows, :])
            s_scr[rows(c), :] = scores
            part = fold(scores, jnp.maximum)
            top = part if top is None else jnp.maximum(top, part)
        top = jnp.max(top, axis=0, keepdims=True)
        size = jnp.zeros((8, ROWS), F32)
        dots = jnp.zeros((8, ROWS), F32)
        for c in range(4):
            weights = jnp.exp(s_scr[rows(c), :] - top)
            grad_weights = nt(vcat[rows(b + c), :], gcat[q_rows, :])
            d_scr[rows(c), :] = grad_weights
            s_scr[rows(c), :] = weights
            size = size + fold(weights, jnp.add)
            dots = dots + fold(weights * grad_weights, jnp.add)
        inverse = 1.0 / jnp.sum(size, axis=0, keepdims=True)
        delta = jnp.sum(dots, axis=0, keepdims=True) * inverse
        dq_t = jnp.zeros((128, ROWS), F32)
        for c in range(4):
            weights = s_scr[rows(c), :] * inverse
            grad_scores = weights * (d_scr[rows(c), :] - delta)
            high = weights.astype(BF16)
            rest = (weights - high.astype(F32)).astype(BF16)
            acc_v[rows(b + c), :] += nn(high, grhs[q_rows, :]) + nn(rest, grhs[q_rows, :])
            high = grad_scores.astype(BF16)
            rest = (grad_scores - high.astype(F32)).astype(BF16)
            acc_k[rows(b + c), :] += nn(high, qrhs[q_rows, :]) + nn(rest, qrhs[q_rows, :])
            keys = kt[:, rows(b + c)]
            dq_t = dq_t + nn(keys, high) + nn(keys, rest)
        dq_t = (dq_t[0:64] + dq_t[64:128]) * SCALE
        dq_scr[q_rows, :] = jnp.concatenate([dq_t, dq_t], axis=0).T
        return carry

    for b in range(4):
        block(b, 0)

    def grad_kv(slot):
        a = acc_k[cells(slot), :]
        b = acc_v[cells(slot), :]
        return jnp.where(low, a + swap_half(a), b + swap_half(b))

    def own_out(s, c, rel, slot):
        here = rel < 16
        x = grad_kv(jnp.where(here, 12 + rel, 0))
        dkv[pl.ds(s * ROWS + c * CELL, CELL), :] = jnp.where(here, x, 0.0)
        x = dq_scr[cells(jnp.where(here, rel, 0)), :]
        half = pl.ds(s * 128 + (c // 2) * CELL, CELL)
        if c % 2 == 0:
            dq[half, :] = x
        else:
            dq[half, :] = jnp.where(low, dq[half, :], x)

    walk(meta, start, total, own_out)

    def before_out(s, c, rel, slot):
        here = rel >= 4
        back[cells(jnp.where(here, slot, HALO)), :] = grad_kv(jnp.where(here, rel - 4, 0))

    walk(meta_prev, start_prev, total, before_out)
    pair = jnp.where(low, dq_scr[cells(came[0]), :], dq_scr[cells(came[1]), :])
    back[pl.ds(HALO * CELL, CELL), :] = pair


def attend(total, info, meta, meta_prev, kv, halo, qg, qgm, m_row):
    kv_rows, qg_rows = ([r for _, r in x] for x in (kv, qg))
    kv, qg = ([x for x, _ in y] for y in (kv, qg))
    shapes = [(4 * ROWS, 128), (2 * ROWS, 128), (HALO * CELL + CELL, 128)]
    keys, queries = 29 * CELL, 17 * CELL
    return pl.pallas_call(
        functools.partial(attend_kernel, total, kv_rows, qg_rows, m_row),
        out_shape=[jax.ShapeDtypeStruct(s, F32) for s in shapes],
        in_specs=[sspec()] * 3 + [vspec()] * 10,
        out_specs=[vspec()] * 3,
        scratch_shapes=[
            VMEM((keys, 512), BF16),
            VMEM((keys, 256), BF16),
            VMEM((128, 28 * CELL), BF16),
            VMEM((28 * CELL, 128), F32),
            VMEM((28 * CELL, 128), F32),
            VMEM((queries, 512), BF16),
            VMEM((queries, 256), BF16),
            VMEM((queries, 128), BF16),
            VMEM((queries, 128), BF16),
            VMEM((queries, 128), F32),
        ]
        + [VMEM((4 * ROWS, ROWS), F32)] * 4,
        compiler_params=params(24),
        cost_estimate=cost(8 << 30, 8 << 20),
        name="attend",
    )(info, meta, meta_prev, *kv, halo, *qg, qgm)


OUT = ROWS + ROWS // 2


def finish_kernel(total, info, meta, dkv, dq, back, *outs):
    low = lanes((CELL, 128)) < 64
    pair = back[pl.ds(HALO * CELL, CELL), :]
    for s in range(PLANE):
        outs[s][pl.ds(ROWS, 128), :] = dq[pl.ds(s * 128, 128), :]

    def visit(s, c, rel, slot):
        out = outs[s]
        sent = rel >= 4
        x = jnp.where(sent, back[cells(jnp.where(sent, slot, 0)), :], 0.0)
        out[pl.ds(c * CELL, CELL), :] = dkv[pl.ds(s * ROWS + c * CELL, CELL), :] + x

        @pl.when(rel >= 16)
        def _():
            straight = (slot - 12) == (c % 2)
            x = jnp.where(straight, pair, swap_half(pair))
            half = pl.ds(ROWS + (c // 2) * CELL, CELL)
            out[half, :] = jnp.where(low == (c % 2 == 0), x, out[half, :])

    walk(meta, info[25], total, visit)


def finish(total, info, meta, dkv, dq, back):
    shapes = [(OUT, 128)] * 4
    return pl.pallas_call(
        functools.partial(finish_kernel, total),
        out_shape=[jax.ShapeDtypeStruct(s, F32) for s in shapes],
        in_specs=[sspec()] * 2 + [vspec()] * 3,
        out_specs=[vspec()] * 4,
        compiler_params=params(),
        cost_estimate=cost(1 << 10, 2 << 20),
        name="finish",
    )(info, meta, dkv, dq, back)


def unpack_kernel(info, *refs):
    parts, (oq, ok, ov) = refs[:12], refs[12:]
    me = info[24]

    def grads(s, c, h):
        return parts[4 * h + s][pl.ds(c * CELL, CELL), :]

    def query(s, c, h):
        x = parts[4 * h + s][pl.ds(ROWS + (c // 2) * CELL, CELL), :]
        return x, swap_half(x)

    for s in range(PLANE):
        j = lax.bitwise_xor(me, s)
        first = pl.ds(pl.multiple_of(j * 128, 128), 128)
        for c in range(CELLS):
            r = pl.ds(c * CELL, CELL)
            a, b = grads(s, c, 0), grads(s, c, 1)
            ok[r, first] = join(a, swap_half(b))
            ov[r, first] = join(swap_half(a), b)
            x0, y0 = query(s, c, 0)
            x1, y1 = query(s, c, 1)
            oq[r, first] = join(x0, y1) if c % 2 == 0 else join(y0, x1)
    for s in (0, 2):
        j = lax.bitwise_xor(me, s)
        even = (j % 2) == 0
        last = pl.ds(pl.multiple_of((4 + j // 2) * 128, 128), 128)
        for c in range(CELLS):
            r = pl.ds(c * CELL, CELL)
            u, w = grads(s, c, 2), grads(s + 1, c, 2)
            a, b = jnp.where(even, u, w), jnp.where(even, w, u)
            ok[r, last] = join(a, swap_half(b))
            ov[r, last] = join(swap_half(a), b)
            u, w = query(s, c, 2)[0], query(s + 1, c, 2)[0]
            a, b = jnp.where(even, u, w), jnp.where(even, w, u)
            oq[r, last] = join(a, swap_half(b)) if c % 2 == 0 else join(swap_half(a), b)


def unpack_heads(info, parts, features):
    return pl.pallas_call(
        unpack_kernel,
        out_shape=[jax.ShapeDtypeStruct((ROWS, features), F32)] * 3,
        in_specs=[sspec()] + [vspec()] * 12,
        out_specs=[vspec()] * 3,
        compiler_params=params(),
        cost_estimate=cost(1 << 20, 5 << 20),
        name="unpack_heads",
    )(info, *[x for part in parts for x in part])


def after(x, *earlier):
    return lax.optimization_barrier((x, *earlier))[0]


def on_device(query_rows, key_rows, value_rows, grad_rows, placement, cell_lengths, gene_mask):
    count = lax.axis_size("ctx")
    total = count * CELLS
    index = lax.axis_index("ctx").astype(jnp.int32)
    plane = index // PLANE

    def along_z(x, step):
        return lax.ppermute(x, "ctx", [(i, (i + step * PLANE) % count) for i in range(count)])

    def swap(x, bit):
        return lax.ppermute(x, "ctx", [(i, i ^ bit) for i in range(count)])

    start = plane * (PLANE * CELLS)
    start_prev = lax.rem(start - PLANE * CELLS + total, total)
    tail = jnp.stack([jnp.int32(0)] * 4 + [index % PLANE, start, start_prev, jnp.int32(0)])
    info = jnp.concatenate([placement, cell_lengths, gene_mask.reshape(-1), tail])

    own0, core0, near0, far0 = pack(
        pack_first_kernel, [(ROWS + 8, 128)] * 4, "pack_first", info, key_rows, value_rows
    )
    near0, far0, core0 = swap(near0, 2), swap(far0, 3), swap(core0, 1)
    sizes = [5 * ROWS] * 2 + [ROWS, 2 * ROWS, 2 * ROWS] * 2
    own, core, *rest = pack(
        pack_rest_kernel,
        [(n, 128) for n in sizes],
        "pack_rest",
        after(info, own0),
        key_rows,
        value_rows,
        query_rows,
        grad_rows,
    )
    near, far = rest[:3], rest[3:]

    def across(i, *earlier):
        pair = (near[i], far[i])
        if earlier:
            pair = after(pair, *earlier)
        near[i], far[i] = swap(pair[0], 2), swap(pair[1], 3)

    across(0)
    first = after((core0, near0, far0), own)
    kv0 = [(x, 0) for x in (own0, *first)]
    meta = jnp.stack([x[ROWS, :32] for x, _ in kv0]).astype(jnp.int32)
    message0 = halo_message(total, info, meta, kv0, None, True)
    halo0 = along_z(message0, 1)
    core = swap(after(core, *first), 1)
    across(1, message0)

    def sources(row0, i, row1):
        return [(own, row0), (core, row0), (near[i], row1), (far[i], row1)]

    qg0 = sources(2 * ROWS, 0, 0)
    movers0 = halo_message(total, info, meta, None, qg0)
    qgm0 = along_z(movers0, 1)
    across(2, movers0)
    kv = [kv0, sources(0, 1, 0), sources(ROWS, 2, 0)]
    qg = [qg0, sources(3 * ROWS, 1, ROWS), sources(4 * ROWS, 2, ROWS)]
    messages = [message0] + [halo_message(total, info, meta, kv[h], qg[h]) for h in (1, 2)]
    halo = [halo0] + [along_z(messages[h], 1) for h in (1, 2)]
    movers = [(qgm0, 0), (halo[1], HALO * CELL), (halo[2], HALO * CELL)]
    meta_prev = halo0[HALO * CELL : HALO * CELL + 4, :32].astype(jnp.int32)

    parts = []
    turn = ()
    for h in range(HEADS):
        came, m_row = movers[h]
        sent = messages[h + 1 :][:1]
        info_h = after(info, *turn, *sent)
        dkv, dq, back = attend(total, info_h, meta, meta_prev, kv[h], halo[h], qg[h], came, m_row)
        turn = (dq,)
        mine, *outs = finish(total, info, meta, dkv, dq, along_z(back, -1))
        parts.append([mine] + [swap(x, i + 1) for i, x in enumerate(outs)])
    return tuple(unpack_heads(info, parts, query_rows.shape[1]))


def solution(mesh):
    rows = P(("groups", "ctx"), None)
    flat = P(("groups", "ctx"))
    return jax.shard_map(
        on_device,
        mesh=mesh,
        in_specs=(rows, rows, rows, rows, flat, flat, rows),
        out_specs=(rows, rows, rows),
        check_vma=False,
    )
```

```python
import functools

import jax
import jax.numpy as jnp
from jax import lax
from jax.experimental import pallas as pl
from jax.experimental.pallas import tpu as pltpu
from jax.sharding import PartitionSpec as P

HEAD_DIM = 64
CELL = 64
CELLS = 4
ROWS = 256
PLANE = 4
HEADS = 3
HALO = 14
ATTEND_COST = 1 << 26
F32 = jnp.float32
BF16 = jnp.bfloat16
VMEM = pltpu.VMEM
NEGATIVE = -1e30
SCALE = HEAD_DIM ** -0.5


def vspec():
    return pl.BlockSpec(memory_space=pltpu.VMEM)


def sspec():
    return pl.BlockSpec(memory_space=pltpu.SMEM)


def params(limit=32):
    return pltpu.CompilerParams(vmem_limit_bytes=limit << 20)


def cost(flops, nbytes):
    return pl.CostEstimate(flops=flops, bytes_accessed=nbytes, transcendentals=0)


def lanes(shape):
    return lax.broadcasted_iota(jnp.int32, shape, 1)


def swap_half(x):
    return pltpu.roll(x, 64, 1)


def join(low, high):
    return jnp.where(lanes(low.shape) < 64, low, high)


def cells(i):
    return pl.ds(pl.multiple_of(i * CELL, CELL), CELL)


def head_blocks(info, c, s, a_ref, b_ref, grads):
    r = pl.ds(c * CELL, CELL)
    j = lax.bitwise_xor(info[24], s)
    first = pl.ds(pl.multiple_of(j * 128, 128), 128)
    last = pl.ds(pl.multiple_of((4 + j // 2) * 128, 128), 128)
    odd = (j % 2) == 1

    def load(lane_tile):
        a, b = a_ref[r, lane_tile], b_ref[r, lane_tile]
        if grads:
            row = lax.broadcasted_iota(jnp.int32, (CELL, 128), 0)
            a, b = a * SCALE, jnp.where(row < info[4 + c], b, 0.0)
        return a, b

    def zero():
        a, b = load(first)
        return join(a, swap_half(b))

    def one():
        a, b = load(first)
        return join(swap_half(a), b)

    def two():
        a, b = load(last)
        return join(jnp.where(odd, swap_half(a), a), jnp.where(odd, b, swap_half(b)))

    return zero, one, two


def pack_kernel(info, k_ref, v_ref, q_ref, g_ref, *outs):
    mine, near, far = outs[:2], outs[2:5], outs[5:8]
    lane = lax.broadcasted_iota(jnp.int32, (8, 128), 1)
    meta = jnp.zeros((8, 128), F32)
    for i in range(20):
        meta = jnp.where(lane == i, info[i].astype(F32), meta)
    for out, row0 in zip((*mine, near[0], far[0]), META_ROWS):
        out[pl.ds(row0, 8), :] = meta
    for s in (2, 3, 1, 0):
        for c in range(CELLS):
            kv = head_blocks(info, c, s, k_ref, v_ref, False)
            qg = head_blocks(info, c, s, q_ref, g_ref, True)
            for h in range(HEADS):
                if s < 2:
                    out, row0 = mine[s], 2 * ROWS * h
                else:
                    out, row0 = (near, far)[s - 2][h], 0
                out[pl.ds(row0 + c * CELL, CELL), :] = kv[h]()
                out[pl.ds(row0 + ROWS + c * CELL, CELL), :] = qg[h]()


META_ROWS = (6 * ROWS, 6 * ROWS, 2 * ROWS, 2 * ROWS)


def pack(kernel, shapes, name, info, *arrays):
    return pl.pallas_call(
        kernel,
        out_shape=[jax.ShapeDtypeStruct(s, F32) for s in shapes],
        in_specs=[sspec()] + [vspec()] * len(arrays),
        out_specs=[vspec()] * len(shapes),
        compiler_params=params(),
        cost_estimate=cost(1 << 20, 3 << 20),
        name=name,
    )(info, *arrays)


def walk(meta, start, total, visit):
    rank = jnp.int32(0)
    for s in range(PLANE):
        for c in range(CELLS):
            rel = lax.rem(meta[s, c] - start + total, total)
            moved = rel >= 16
            slot = jnp.where(moved, 12 + rank, rel - 4)
            visit(s, c, rel, slot)
            rank = rank + moved.astype(jnp.int32)


def halo_kernel(total, h, info, meta, *refs):
    parts, out = refs[:4], refs[4]

    def visit(s, c, rel, slot):
        @pl.when(rel >= 4)
        def _():
            out[cells(slot), :] = parts[s][pl.ds(KV_ROWS[h][s] + c * CELL, CELL), :]

        @pl.when(rel >= 16)
        def _():
            out[cells(slot + 2), :] = parts[s][pl.ds(QG_ROWS[h][s] + c * CELL, CELL), :]

    walk(meta, info[25], total, visit)
    if h == 0:
        out[pl.ds((HALO + 2) * CELL, 8), :] = jnp.zeros((8, 128), F32)
        for s in range(PLANE):
            out[pl.ds((HALO + 2) * CELL + s, 1), :] = parts[s][pl.ds(META_ROWS[s], 1), :]


KV_ROWS = tuple((2 * h * ROWS, 2 * h * ROWS, 0, 0) for h in range(HEADS))
QG_ROWS = tuple(tuple(r + ROWS for r in rows) for rows in KV_ROWS)


def halo_message(total, h, info, meta, parts):
    rows = (HALO + 2) * CELL + (8 if h == 0 else 0)
    return pl.pallas_call(
        functools.partial(halo_kernel, total, h),
        out_shape=jax.ShapeDtypeStruct((rows, 128), F32),
        in_specs=[sspec()] * 2 + [vspec()] * 4,
        out_specs=vspec(),
        compiler_params=params(),
        cost_estimate=cost(1 << 10, 1 << 20),
        name="halo_message",
    )(info, meta, *parts)


def split(x):
    high = x.astype(BF16).astype(F32)
    return high, x - high


def nt(a, b):
    return lax.dot_general(a, b, (((1,), (1,)), ((), ())), preferred_element_type=F32)


def nn(a, b):
    return lax.dot_general(a, b, (((1,), (0,)), ((), ())), preferred_element_type=F32)


def tn(a, b):
    return lax.dot_general(a, b, (((0,), (0,)), ((), ())), preferred_element_type=F32)


def attend_kernel(total, h, info, meta, meta_prev, *refs):
    here_parts, halo = refs[:4], refs[4]
    dkv, dq, back = refs[5:8]
    kcat, vcat, kt, acc_k, acc_v, qcat, gcat, qrhs, grhs, dq_scr = refs[8:18]
    pairs = (refs[18:20], refs[20:22])
    start = info[25]
    start_prev = info[26]
    lane = lax.broadcasted_iota(jnp.int32, (CELL, 128), 1)
    low = lane < 64
    lane16 = lax.broadcasted_iota(jnp.int32, (16, 128), 1)
    row16 = lax.broadcasted_iota(jnp.int32, (16, 128), 0)

    def put_key(x, slot, m, s, c):
        length = m[s, 4 + c]
        parts = []
        for i in range(4):
            limit = length - 16 * i
            if i > 0:
                limit = jnp.where(m[s, 7 + 3 * c + i] > 0, 0, limit)
            parts.append(jnp.where((row16 >= limit) & (lane16 == 64), NEGATIVE, 0.0))
        bias = jnp.concatenate(parts, axis=0)
        high, rest = split(x)
        high_r, rest_r = swap_half(high), swap_half(rest)
        mid, least = split(rest)
        kcat[cells(slot), pl.ds(0, 128)] = jnp.where(low, high, rest_r).astype(BF16)
        kcat[cells(slot), pl.ds(128, 128)] = jnp.where(low, high, bias).astype(BF16)
        kcat[cells(slot), pl.ds(256, 128)] = jnp.where(low, mid, swap_half(least)).astype(BF16)
        kcat[cells(slot), pl.ds(384, 128)] = jnp.where(low, high, 0.0).astype(BF16)
        vcat[cells(slot), pl.ds(0, 128)] = jnp.where(low, high_r, rest).astype(BF16)
        vcat[cells(slot), pl.ds(128, 128)] = jnp.where(low, high_r, 0.0).astype(BF16)

    one = jnp.where(lane == 64, 1.0, 0.0)

    def put_query(x, slot):
        high, rest = split(x)
        high_r, rest_r = swap_half(high), swap_half(rest)
        qcat[cells(slot), pl.ds(0, 128)] = jnp.where(low, high, high_r).astype(BF16)
        qcat[cells(slot), pl.ds(128, 128)] = jnp.where(low, rest, one).astype(BF16)
        mid, least = split(rest)
        qcat[cells(slot), pl.ds(256, 128)] = jnp.where(low, mid, high_r).astype(BF16)
        qcat[cells(slot), pl.ds(384, 128)] = jnp.where(low, least, 0.0).astype(BF16)
        gcat[cells(slot), pl.ds(0, 128)] = jnp.where(low, high_r, high).astype(BF16)
        gcat[cells(slot), pl.ds(128, 128)] = jnp.where(low, rest_r, 0.0).astype(BF16)
        qrhs[cells(slot), :] = jnp.where(low, high, rest_r).astype(BF16)
        grhs[cells(slot), :] = jnp.where(low, rest_r, high).astype(BF16)

    def own(s, c, rel, slot):
        here = rel < 16
        put_key(here_parts[s][pl.ds(KV_ROWS[h][s] + c * CELL, CELL), :], jnp.where(here, 12 + rel, 28), meta, s, c)
        put_query(here_parts[s][pl.ds(QG_ROWS[h][s] + c * CELL, CELL), :], jnp.where(here, rel, 16))

    walk(meta, start, total, own)
    came = [jnp.int32(0), jnp.int32(0)]

    def before(s, c, rel, slot):
        here = rel >= 4
        x = halo[cells(jnp.where(here, slot, 0)), :]
        put_key(x, jnp.where(here, rel - 4, 28), meta_prev, s, c)
        for i in range(2):
            came[i] = jnp.where((rel >= 16) & (slot == 12 + i), rel - 16, came[i])

    walk(meta_prev, start_prev, total, before)
    for i in range(2):
        put_query(halo[pl.ds((HALO + i) * CELL, CELL), :], came[i])
    for j in range(7):
        kt[:, pl.ds(j * ROWS, ROWS)] = kcat[pl.ds(j * ROWS, ROWS), pl.ds(0, 128)].T
    acc_k[...] = jnp.zeros(acc_k.shape, F32)
    acc_v[...] = jnp.zeros(acc_v.shape, F32)

    def fold(x, op):
        out = x[0:8]
        for i in range(1, x.shape[0] // 8):
            out = op(out, x[8 * i : 8 * i + 8])
        return out

    def block(b, carry):
        s_scr, d_scr = pairs[b % 2 if isinstance(b, int) else 0]

        def rows(i, n=ROWS):
            return pl.ds(i * ROWS if isinstance(i, int) else pl.multiple_of(i * ROWS, ROWS), n)

        q_rows = rows(b)
        top = None
        for c in range(4):
            scores = nt(kcat[rows(b + c), :], qcat[q_rows, :])
            s_scr[rows(c), :] = scores
            part = fold(scores, jnp.maximum)
            top = part if top is None else jnp.maximum(top, part)
        top = jnp.max(top, axis=0, keepdims=True)
        size = jnp.zeros((8, ROWS), F32)
        dots = jnp.zeros((8, ROWS), F32)
        for c in range(4):
            weights = jnp.exp(s_scr[rows(c), :] - top)
            grad_weights = nt(vcat[rows(b + c), :], gcat[q_rows, :])
            d_scr[rows(c), :] = grad_weights
            s_scr[rows(c), :] = weights
            size = size + fold(weights, jnp.add)
            dots = dots + fold(weights * grad_weights, jnp.add)
        inverse = 1.0 / jnp.sum(size, axis=0, keepdims=True)
        delta = jnp.sum(dots, axis=0, keepdims=True) * inverse
        dq_t = jnp.zeros((128, ROWS), F32)
        for c in range(4):
            weights = s_scr[rows(c), :] * inverse
            grad_scores = weights * (d_scr[rows(c), :] - delta)
            high = weights.astype(BF16)
            rest = (weights - high.astype(F32)).astype(BF16)
            acc_v[rows(b + c), :] += nn(high, grhs[q_rows, :]) + nn(rest, grhs[q_rows, :])
            high = grad_scores.astype(BF16)
            rest = (grad_scores - high.astype(F32)).astype(BF16)
            acc_k[rows(b + c), :] += nn(high, qrhs[q_rows, :]) + nn(rest, qrhs[q_rows, :])
            keys = kt[:, rows(b + c)]
            dq_t = dq_t + nn(keys, high) + nn(keys, rest)
        dq_t = (dq_t[0:64] + dq_t[64:128]) * SCALE
        dq_scr[q_rows, :] = jnp.concatenate([dq_t, dq_t], axis=0).T
        return carry

    for b in range(4):
        block(b, 0)

    def grad_kv(slot):
        a = acc_k[cells(slot), :]
        b = acc_v[cells(slot), :]
        return jnp.where(low, a + swap_half(a), b + swap_half(b))

    def own_out(s, c, rel, slot):
        here = rel < 16
        x = grad_kv(jnp.where(here, 12 + rel, 0))
        dkv[pl.ds(s * ROWS + c * CELL, CELL), :] = jnp.where(here, x, 0.0)
        x = dq_scr[cells(jnp.where(here, rel, 0)), :]
        half = pl.ds(s * 128 + (c // 2) * CELL, CELL)
        if c % 2 == 0:
            dq[half, :] = x
        else:
            dq[half, :] = jnp.where(low, dq[half, :], x)

    walk(meta, start, total, own_out)

    def before_out(s, c, rel, slot):
        here = rel >= 4
        back[cells(jnp.where(here, slot, HALO)), :] = grad_kv(jnp.where(here, rel - 4, 0))

    walk(meta_prev, start_prev, total, before_out)
    pair = jnp.where(low, dq_scr[cells(came[0]), :], dq_scr[cells(came[1]), :])
    back[pl.ds(HALO * CELL, CELL), :] = pair


def attend(total, h, info, meta, meta_prev, parts, halo):
    shapes = [(4 * ROWS, 128), (2 * ROWS, 128), (HALO * CELL + CELL, 128)]
    keys, queries = 29 * CELL, 17 * CELL
    return pl.pallas_call(
        functools.partial(attend_kernel, total, h),
        out_shape=[jax.ShapeDtypeStruct(s, F32) for s in shapes],
        in_specs=[sspec()] * 3 + [vspec()] * 5,
        out_specs=[vspec()] * 3,
        scratch_shapes=[
            VMEM((keys, 512), BF16),
            VMEM((keys, 256), BF16),
            VMEM((128, 28 * CELL), BF16),
            VMEM((28 * CELL, 128), F32),
            VMEM((28 * CELL, 128), F32),
            VMEM((queries, 512), BF16),
            VMEM((queries, 256), BF16),
            VMEM((queries, 128), BF16),
            VMEM((queries, 128), BF16),
            VMEM((queries, 128), F32),
        ]
        + [VMEM((4 * ROWS, ROWS), F32)] * 4,
        compiler_params=params(24),
        cost_estimate=cost(ATTEND_COST, 1 << 20),
        name="attend",
    )(info, meta, meta_prev, *parts, halo)


OUT = ROWS + ROWS // 2


def finish_kernel(total, n, info, meta, dkv, dq, back, *refs):
    earlier, outs = refs[:n], refs[n:]
    for i in range(n):
        outs[1][pl.ds((i + 1) * OUT, OUT), :] = earlier[i][...]
    low = lanes((CELL, 128)) < 64
    pair = back[pl.ds(HALO * CELL, CELL), :]
    for s in range(PLANE):
        outs[s][pl.ds(ROWS, 128), :] = dq[pl.ds(s * 128, 128), :]

    def visit(s, c, rel, slot):
        out = outs[s]
        sent = rel >= 4
        x = jnp.where(sent, back[cells(jnp.where(sent, slot, 0)), :], 0.0)
        out[pl.ds(c * CELL, CELL), :] = dkv[pl.ds(s * ROWS + c * CELL, CELL), :] + x

        @pl.when(rel >= 16)
        def _():
            straight = (slot - 12) == (c % 2)
            x = jnp.where(straight, pair, swap_half(pair))
            half = pl.ds(ROWS + (c // 2) * CELL, CELL)
            out[half, :] = jnp.where(low == (c % 2 == 0), x, out[half, :])

    walk(meta, info[25], total, visit)


def finish(total, info, meta, dkv, dq, back, earlier):
    n = len(earlier)
    shapes = [(OUT, 128), (OUT * (n + 1), 128), (OUT, 128), (OUT, 128)]
    return pl.pallas_call(
        functools.partial(finish_kernel, total, n),
        out_shape=[jax.ShapeDtypeStruct(s, F32) for s in shapes],
        in_specs=[sspec()] * 2 + [vspec()] * (3 + n),
        out_specs=[vspec()] * 4,
        compiler_params=params(),
        cost_estimate=cost(1 << 10, 2 << 20),
        name="finish",
    )(info, meta, dkv, dq, back, *earlier)


def unpack_kernel(info, *refs):
    core, heads, (oq, ok, ov) = refs[0], refs[1:10], refs[10:]
    me = info[24]
    core_row = (OUT, 2 * OUT, 0)
    step = pl.program_id(0)

    def rows(s, h, row):
        if s == 1:
            return core[pl.ds(pl.multiple_of(core_row[h] + row, CELL), CELL), :]
        return heads[3 * h + (0, None, 1, 2)[s]][pl.ds(pl.multiple_of(row, CELL), CELL), :]

    def grads(s, c, h):
        return rows(s, h, (2 * step + c) * CELL)

    def query(s, c, h):
        x = rows(s, h, ROWS + step * CELL)
        return x, swap_half(x)

    for s in range(PLANE):
        j = lax.bitwise_xor(me, s)
        first = pl.ds(pl.multiple_of(j * 128, 128), 128)
        for c in range(2):
            r = pl.ds(c * CELL, CELL)
            a, b = grads(s, c, 0), grads(s, c, 1)
            ok[r, first] = join(a, swap_half(b))
            ov[r, first] = join(swap_half(a), b)
            x0, y0 = query(s, c, 0)
            x1, y1 = query(s, c, 1)
            oq[r, first] = join(x0, y1) if c % 2 == 0 else join(y0, x1)
    for s in (0, 2):
        j = lax.bitwise_xor(me, s)
        even = (j % 2) == 0
        last = pl.ds(pl.multiple_of((4 + j // 2) * 128, 128), 128)
        for c in range(2):
            r = pl.ds(c * CELL, CELL)
            u, w = grads(s, c, 2), grads(s + 1, c, 2)
            a, b = jnp.where(even, u, w), jnp.where(even, w, u)
            ok[r, last] = join(a, swap_half(b))
            ov[r, last] = join(swap_half(a), b)
            u, w = query(s, c, 2)[0], query(s + 1, c, 2)[0]
            a, b = jnp.where(even, u, w), jnp.where(even, w, u)
            oq[r, last] = join(a, swap_half(b)) if c % 2 == 0 else join(swap_half(a), b)


def unpack_heads(info, core, parts, features):
    return pl.pallas_call(
        unpack_kernel,
        out_shape=[jax.ShapeDtypeStruct((ROWS, features), F32)] * 3,
        grid=(2,),
        in_specs=[sspec()] + [vspec()] * 10,
        out_specs=[pl.BlockSpec((ROWS // 2, features), lambda i: (i, 0))] * 3,
        compiler_params=params(),
        cost_estimate=cost(1 << 20, 5 << 20),
        name="unpack_heads",
    )(info, core, *[x for part in parts for x in part])


def after(x, *earlier):
    return lax.optimization_barrier((x, *earlier))[0]


def on_device(query_rows, key_rows, value_rows, grad_rows, placement, cell_lengths, gene_mask):
    count = lax.axis_size("ctx")
    total = count * CELLS
    index = lax.axis_index("ctx").astype(jnp.int32)
    plane = index // PLANE

    def along_z(x, step):
        return lax.ppermute(x, "ctx", [(i, (i + step * PLANE) % count) for i in range(count)])

    def swap(x, bit):
        return lax.ppermute(x, "ctx", [(i, i ^ bit) for i in range(count)])

    start = plane * (PLANE * CELLS)
    start_prev = lax.rem(start - PLANE * CELLS + total, total)
    tail = jnp.stack([jnp.int32(0)] * 4 + [index % PLANE, start, start_prev, jnp.int32(0)])
    info = jnp.concatenate([placement, cell_lengths, gene_mask.reshape(-1), tail])

    sizes = [6 * ROWS + 8] * 2 + [2 * ROWS + 8, 2 * ROWS, 2 * ROWS] * 2
    shapes = [(n, 128) for n in sizes]
    arrays = (key_rows, value_rows, query_rows, grad_rows)
    own, core, *rest = pack(pack_kernel, shapes, "pack_heads", info, *arrays)
    near, far = rest[:3], rest[3:]

    def across(h, *earlier):
        pair = (near[h], far[h])
        if earlier:
            pair = after(pair, *earlier)
        near[h], far[h] = swap(pair[0], 2), swap(pair[1], 3)

    across(0)
    core = swap(core, 1)
    across(1, core)
    first = (own, core, near[0], far[0])
    meta = jnp.stack([x[r, :32] for x, r in zip(first, META_ROWS)]).astype(jnp.int32)
    message = halo_message(total, 0, info, meta, first)
    halo = [along_z(message, 1)]
    across(2, message)
    corner = (HALO + 2) * CELL
    meta_prev = halo[0][corner : corner + 4, :32].astype(jnp.int32)
    dkv, dq, back = [], [], []
    for h in range(HEADS):
        earlier = [*dq[-1:], message]
        if h < HEADS - 1:
            held = (own, core, near[h + 1], far[h + 1])
            message = halo_message(total, h + 1, after(info, *dq[-1:]), meta, held)
            halo.append(along_z(message, 1))
            earlier.append(message)
        held = (own, core, near[h], far[h])
        outs = attend(total, h, after(info, *earlier), meta, meta_prev, held, halo[h])
        dkv.append(outs[0])
        dq.append(outs[1])
        back.append(along_z(outs[2], -1))

    parts, cores = [], []

    def finish_head(h):
        earlier = cores[:] if h == HEADS - 1 else []
        info_h = after(info, *(parts[-1][1:] if parts else dq[2:]))
        mine, core, near, far = finish(total, info_h, meta, dkv[h], dq[h], back[h], earlier)
        cores.append(core)
        parts.append((mine, swap(near, 2), swap(far, 3)))

    for h in range(HEADS):
        finish_head(h)
    return tuple(unpack_heads(info, swap(cores[-1], 1), parts, query_rows.shape[1]))


def solution(mesh):
    rows = P(("groups", "ctx"), None)
    flat = P(("groups", "ctx"))
    return jax.shard_map(
        on_device,
        mesh=mesh,
        in_specs=(rows, rows, rows, rows, flat, flat, rows),
        out_specs=(rows, rows, rows),
        check_vma=False,
    )
```

```python
import functools

import jax
import jax.numpy as jnp
from jax import lax
from jax.experimental import pallas as pl
from jax.experimental.pallas import tpu as pltpu
from jax.sharding import PartitionSpec as P

HEAD_DIM = 64
CELL = 64
CELLS = 4
ROWS = 256
PLANE = 4
HEADS = 3
HALO = 14
ATTEND_COST = 1 << 26
BLOCK = 16
KEPT = 43
F32 = jnp.float32
BF16 = jnp.bfloat16
VMEM = pltpu.VMEM
NEGATIVE = -1e30
SCALE = HEAD_DIM ** -0.5


def vspec():
    return pl.BlockSpec(memory_space=pltpu.VMEM)


def sspec():
    return pl.BlockSpec(memory_space=pltpu.SMEM)


def params(limit=32):
    return pltpu.CompilerParams(vmem_limit_bytes=limit << 20)


def cost(flops, nbytes):
    return pl.CostEstimate(flops=flops, bytes_accessed=nbytes, transcendentals=0)


def lanes(shape):
    return lax.broadcasted_iota(jnp.int32, shape, 1)


def swap_half(x):
    return pltpu.roll(x, 64, 1)


def join(low, high):
    return jnp.where(lanes(low.shape) < 64, low, high)


def cells(i):
    return pl.ds(pl.multiple_of(i * CELL, CELL), CELL)


def head_blocks(info, c, s, a_ref, b_ref, grads):
    r = pl.ds(c * CELL, CELL)
    j = lax.bitwise_xor(info[24], s)
    first = pl.ds(pl.multiple_of(j * 128, 128), 128)
    last = pl.ds(pl.multiple_of((4 + j // 2) * 128, 128), 128)
    odd = (j % 2) == 1

    def load(lane_tile):
        a, b = a_ref[r, lane_tile], b_ref[r, lane_tile]
        if grads:
            row = lax.broadcasted_iota(jnp.int32, (CELL, 128), 0)
            a, b = a * SCALE, jnp.where(row < info[4 + c], b, 0.0)
        return a, b

    def zero():
        a, b = load(first)
        return join(a, swap_half(b))

    def one():
        a, b = load(first)
        return join(swap_half(a), b)

    def two():
        a, b = load(last)
        return join(jnp.where(odd, swap_half(a), a), jnp.where(odd, b, swap_half(b)))

    return zero, one, two


def pack_kernel(info, k_ref, v_ref, q_ref, g_ref, *outs):
    mine, near, far = outs[:2], outs[2:5], outs[5:8]
    lane = lax.broadcasted_iota(jnp.int32, (8, 128), 1)
    meta = jnp.zeros((8, 128), F32)
    for i in range(20):
        meta = jnp.where(lane == i, info[i].astype(F32), meta)
    for out, row0 in zip((*mine, near[0], far[0]), META_ROWS):
        out[pl.ds(row0, 8), :] = meta
    for s in (2, 3, 1, 0):
        for c in range(CELLS):
            kv = head_blocks(info, c, s, k_ref, v_ref, False)
            qg = head_blocks(info, c, s, q_ref, g_ref, True)
            for h in range(HEADS):
                if s < 2:
                    out, row0 = mine[s], 2 * ROWS * h
                else:
                    out, row0 = (near, far)[s - 2][h], 0
                out[pl.ds(row0 + c * CELL, CELL), :] = kv[h]()
                out[pl.ds(row0 + ROWS + c * CELL, CELL), :] = qg[h]()


META_ROWS = (6 * ROWS, 6 * ROWS, 2 * ROWS, 2 * ROWS)


def pack(kernel, shapes, name, info, *arrays):
    return pl.pallas_call(
        kernel,
        out_shape=[jax.ShapeDtypeStruct(s, F32) for s in shapes],
        in_specs=[sspec()] + [vspec()] * len(arrays),
        out_specs=[vspec()] * len(shapes),
        compiler_params=params(),
        cost_estimate=cost(1 << 20, 3 << 20),
        name=name,
    )(info, *arrays)


def walk(meta, start, total, visit, kept=None):
    rank, count = jnp.int32(0), jnp.int32(0)
    for s in range(PLANE):
        for c in range(CELLS):
            rel = lax.rem(meta[s, c] - start + total, total)
            moved = rel >= 16
            slot = jnp.where(moved, 12 + rank, rel - 4)
            at = []
            for i in range(4 if kept else 0):
                seen = (rel >= 4) & (meta[s, 4 + c] > BLOCK * i)
                if i > 0:
                    seen = seen & (meta[s, 7 + 3 * c + i] == 0)
                at.append((seen, jnp.where(seen, jnp.minimum(count, kept), kept)))
                count = count + seen.astype(jnp.int32)
            visit(s, c, rel, slot, at)
            rank = rank + moved.astype(jnp.int32)
    return count


def span(kept):
    return (kept + 1) * BLOCK // CELL if kept else HALO


def block16(i):
    return pl.ds(pl.multiple_of(i * BLOCK, BLOCK), BLOCK)


def halo_kernel(total, h, kept, info, meta, *refs):
    parts, out = refs[:4], refs[-1]
    first = span(kept)
    if kept:
        out[block16(kept), :] = jnp.zeros((BLOCK, 128), F32)

    def visit(s, c, rel, slot, at):
        row0 = KV_ROWS[h][s] + c * CELL
        for i, (_, place) in enumerate(at):
            out[block16(place), :] = parts[s][pl.ds(row0 + BLOCK * i, BLOCK), :]
        if not kept:

            @pl.when(rel >= 4)
            def _():
                out[cells(slot), :] = parts[s][pl.ds(row0, CELL), :]

        @pl.when(rel >= 16)
        def _():
            out[cells(first + slot - 12), :] = parts[s][pl.ds(QG_ROWS[h][s] + c * CELL, CELL), :]

    count = walk(meta, info[25], total, visit, kept)
    if kept or h == 0:
        out[pl.ds((first + 2) * CELL, 8), :] = jnp.zeros((8, 128), F32)
        for s in range(PLANE if h == 0 else 0):
            out[pl.ds((first + 2) * CELL + s, 1), :] = parts[s][pl.ds(META_ROWS[s], 1), :]
    if kept:
        at = pl.ds((first + 2) * CELL + PLANE, 1)
        flag = jnp.full((1, 128), (count > kept).astype(F32))
        for came in refs[4:-1]:
            flag = jnp.maximum(flag, came[at, :])
        out[at, :] = flag


KV_ROWS = tuple((2 * h * ROWS, 2 * h * ROWS, 0, 0) for h in range(HEADS))
QG_ROWS = tuple(tuple(r + ROWS for r in rows) for rows in KV_ROWS)


def halo_message(total, h, kept, info, meta, parts, came):
    came = came[-1:] if kept else []
    rows = (span(kept) + 2) * CELL + (8 if kept or h == 0 else 0)
    return pl.pallas_call(
        functools.partial(halo_kernel, total, h, kept),
        out_shape=jax.ShapeDtypeStruct((rows, 128), F32),
        in_specs=[sspec()] * 2 + [vspec()] * (4 + len(came)),
        out_specs=vspec(),
        compiler_params=params(),
        cost_estimate=cost(1 << 10, 1 << 20),
        name="halo_message",
    )(info, meta, *parts, *came)


def split(x):
    high = x.astype(BF16).astype(F32)
    return high, x - high


def nt(a, b):
    return lax.dot_general(a, b, (((1,), (1,)), ((), ())), preferred_element_type=F32)


def nn(a, b):
    return lax.dot_general(a, b, (((1,), (0,)), ((), ())), preferred_element_type=F32)


def tn(a, b):
    return lax.dot_general(a, b, (((0,), (0,)), ((), ())), preferred_element_type=F32)


def attend_kernel(total, h, kept, info, meta, meta_prev, *refs):
    here_parts, halo = refs[:4], refs[4]
    dkv, dq, back = refs[5:8]
    kcat, vcat, kt, acc_k, acc_v, qcat, gcat, qrhs, grhs, dq_scr = refs[8:18]
    pairs = (refs[18:20], refs[20:22])
    start = info[25]
    start_prev = info[26]
    lane = lax.broadcasted_iota(jnp.int32, (CELL, 128), 1)
    low = lane < 64
    lane16 = lax.broadcasted_iota(jnp.int32, (16, 128), 1)
    row16 = lax.broadcasted_iota(jnp.int32, (16, 128), 0)

    def put_key(x, slot, m, s, c):
        length = m[s, 4 + c]
        parts = []
        for i in range(4):
            limit = length - 16 * i
            if i > 0:
                limit = jnp.where(m[s, 7 + 3 * c + i] > 0, 0, limit)
            parts.append(jnp.where((row16 >= limit) & (lane16 == 64), NEGATIVE, 0.0))
        bias = jnp.concatenate(parts, axis=0)
        high, rest = split(x)
        high_r, rest_r = swap_half(high), swap_half(rest)
        mid, least = split(rest)
        kcat[cells(slot), pl.ds(0, 128)] = jnp.where(low, high, rest_r).astype(BF16)
        kcat[cells(slot), pl.ds(128, 128)] = jnp.where(low, high, bias).astype(BF16)
        kcat[cells(slot), pl.ds(256, 128)] = jnp.where(low, mid, swap_half(least)).astype(BF16)
        kcat[cells(slot), pl.ds(384, 128)] = jnp.where(low, high, 0.0).astype(BF16)
        vcat[cells(slot), pl.ds(0, 128)] = jnp.where(low, high_r, rest).astype(BF16)
        vcat[cells(slot), pl.ds(128, 128)] = jnp.where(low, high_r, 0.0).astype(BF16)

    one = jnp.where(lane == 64, 1.0, 0.0)

    def put_query(x, slot):
        high, rest = split(x)
        high_r, rest_r = swap_half(high), swap_half(rest)
        qcat[cells(slot), pl.ds(0, 128)] = jnp.where(low, high, high_r).astype(BF16)
        qcat[cells(slot), pl.ds(128, 128)] = jnp.where(low, rest, one).astype(BF16)
        mid, least = split(rest)
        qcat[cells(slot), pl.ds(256, 128)] = jnp.where(low, mid, high_r).astype(BF16)
        qcat[cells(slot), pl.ds(384, 128)] = jnp.where(low, least, 0.0).astype(BF16)
        gcat[cells(slot), pl.ds(0, 128)] = jnp.where(low, high_r, high).astype(BF16)
        gcat[cells(slot), pl.ds(128, 128)] = jnp.where(low, rest_r, 0.0).astype(BF16)
        qrhs[cells(slot), :] = jnp.where(low, high, rest_r).astype(BF16)
        grhs[cells(slot), :] = jnp.where(low, rest_r, high).astype(BF16)

    def own(s, c, rel, slot, at):
        here = rel < 16
        put_key(here_parts[s][pl.ds(KV_ROWS[h][s] + c * CELL, CELL), :], jnp.where(here, 12 + rel, 28), meta, s, c)
        put_query(here_parts[s][pl.ds(QG_ROWS[h][s] + c * CELL, CELL), :], jnp.where(here, rel, 16))

    walk(meta, start, total, own)
    came = [jnp.int32(0), jnp.int32(0)]

    def before(s, c, rel, slot, at):
        here = rel >= 4
        if kept:
            x = jnp.concatenate([halo[block16(place), :] for _, place in at], axis=0)
        else:
            x = halo[cells(jnp.where(here, slot, 0)), :]
        put_key(x, jnp.where(here, rel - 4, 28), meta_prev, s, c)
        for i in range(2):
            came[i] = jnp.where((rel >= 16) & (slot == 12 + i), rel - 16, came[i])

    walk(meta_prev, start_prev, total, before, kept)
    for i in range(2):
        put_query(halo[pl.ds((span(kept) + i) * CELL, CELL), :], came[i])
    for j in range(7):
        kt[:, pl.ds(j * ROWS, ROWS)] = kcat[pl.ds(j * ROWS, ROWS), pl.ds(0, 128)].T
    acc_k[...] = jnp.zeros(acc_k.shape, F32)
    acc_v[...] = jnp.zeros(acc_v.shape, F32)

    def fold(x, op):
        out = x[0:8]
        for i in range(1, x.shape[0] // 8):
            out = op(out, x[8 * i : 8 * i + 8])
        return out

    def block(b, carry):
        s_scr, d_scr = pairs[b % 2 if isinstance(b, int) else 0]

        def rows(i, n=ROWS):
            return pl.ds(i * ROWS if isinstance(i, int) else pl.multiple_of(i * ROWS, ROWS), n)

        q_rows = rows(b)
        top = None
        for c in range(4):
            scores = nt(kcat[rows(b + c), :], qcat[q_rows, :])
            s_scr[rows(c), :] = scores
            part = fold(scores, jnp.maximum)
            top = part if top is None else jnp.maximum(top, part)
        top = jnp.max(top, axis=0, keepdims=True)
        size = jnp.zeros((8, ROWS), F32)
        dots = jnp.zeros((8, ROWS), F32)
        for c in range(4):
            weights = jnp.exp(s_scr[rows(c), :] - top)
            grad_weights = nt(vcat[rows(b + c), :], gcat[q_rows, :])
            d_scr[rows(c), :] = grad_weights
            s_scr[rows(c), :] = weights
            size = size + fold(weights, jnp.add)
            dots = dots + fold(weights * grad_weights, jnp.add)
        inverse = 1.0 / jnp.sum(size, axis=0, keepdims=True)
        delta = jnp.sum(dots, axis=0, keepdims=True) * inverse
        dq_t = jnp.zeros((128, ROWS), F32)
        for c in range(4):
            weights = s_scr[rows(c), :] * inverse
            grad_scores = weights * (d_scr[rows(c), :] - delta)
            high = weights.astype(BF16)
            rest = (weights - high.astype(F32)).astype(BF16)
            acc_v[rows(b + c), :] += nn(high, grhs[q_rows, :]) + nn(rest, grhs[q_rows, :])
            high = grad_scores.astype(BF16)
            rest = (grad_scores - high.astype(F32)).astype(BF16)
            acc_k[rows(b + c), :] += nn(high, qrhs[q_rows, :]) + nn(rest, qrhs[q_rows, :])
            keys = kt[:, rows(b + c)]
            dq_t = dq_t + nn(keys, high) + nn(keys, rest)
        dq_t = (dq_t[0:64] + dq_t[64:128]) * SCALE
        dq_scr[q_rows, :] = jnp.concatenate([dq_t, dq_t], axis=0).T
        return carry

    if kept:
        for b in range(4):
            block(b, 0)
    else:
        lax.fori_loop(0, 4, block, 0)

    def grad_kv(slot):
        a = acc_k[cells(slot), :]
        b = acc_v[cells(slot), :]
        return jnp.where(low, a + swap_half(a), b + swap_half(b))

    def own_out(s, c, rel, slot, at):
        here = rel < 16
        x = grad_kv(jnp.where(here, 12 + rel, 0))
        dkv[pl.ds(s * ROWS + c * CELL, CELL), :] = jnp.where(here, x, 0.0)
        x = dq_scr[cells(jnp.where(here, rel, 0)), :]
        half = pl.ds(s * 128 + (c // 2) * CELL, CELL)
        if c % 2 == 0:
            dq[half, :] = x
        else:
            dq[half, :] = jnp.where(low, dq[half, :], x)

    walk(meta, start, total, own_out)

    def before_out(s, c, rel, slot, at):
        here = rel >= 4
        x = grad_kv(jnp.where(here, rel - 4, 0))
        for i, (_, place) in enumerate(at):
            back[block16(place), :] = x[BLOCK * i : BLOCK * (i + 1)]
        if not kept:
            back[cells(jnp.where(here, slot, HALO)), :] = x

    walk(meta_prev, start_prev, total, before_out, kept)
    pair = jnp.where(low, dq_scr[cells(came[0]), :], dq_scr[cells(came[1]), :])
    back[pl.ds(span(kept) * CELL, CELL), :] = pair


def attend(total, h, kept, info, meta, meta_prev, parts, halo):
    shapes = [(4 * ROWS, 128), (2 * ROWS, 128), ((span(kept) + 1) * CELL, 128)]
    keys, queries = 29 * CELL, 17 * CELL
    return pl.pallas_call(
        functools.partial(attend_kernel, total, h, kept),
        out_shape=[jax.ShapeDtypeStruct(s, F32) for s in shapes],
        in_specs=[sspec()] * 3 + [vspec()] * 5,
        out_specs=[vspec()] * 3,
        scratch_shapes=[
            VMEM((keys, 512), BF16),
            VMEM((keys, 256), BF16),
            VMEM((128, 28 * CELL), BF16),
            VMEM((28 * CELL, 128), F32),
            VMEM((28 * CELL, 128), F32),
            VMEM((queries, 512), BF16),
            VMEM((queries, 256), BF16),
            VMEM((queries, 128), BF16),
            VMEM((queries, 128), BF16),
            VMEM((queries, 128), F32),
        ]
        + [VMEM((4 * ROWS, ROWS), F32)] * 4,
        compiler_params=params(24),
        cost_estimate=cost(ATTEND_COST, 1 << 20),
        name="attend",
    )(info, meta, meta_prev, *parts, halo)


OUT = ROWS + ROWS // 2


def finish_kernel(total, n, kept, info, meta, dkv, dq, back, *refs):
    earlier, outs = refs[:n], refs[n:]
    for i in range(n):
        outs[1][pl.ds((i + 1) * OUT, OUT), :] = earlier[i][...]
    low = lanes((CELL, 128)) < 64
    pair = back[pl.ds(span(kept) * CELL, CELL), :]
    for s in range(PLANE):
        outs[s][pl.ds(ROWS, 128), :] = dq[pl.ds(s * 128, 128), :]

    def visit(s, c, rel, slot, at):
        out = outs[s]
        sent = rel >= 4
        if kept:
            x = [jnp.where(seen, back[block16(place), :], 0.0) for seen, place in at]
            x = jnp.concatenate(x, axis=0)
        else:
            x = jnp.where(sent, back[cells(jnp.where(sent, slot, 0)), :], 0.0)
        out[pl.ds(c * CELL, CELL), :] = dkv[pl.ds(s * ROWS + c * CELL, CELL), :] + x

        @pl.when(rel >= 16)
        def _():
            straight = (slot - 12) == (c % 2)
            x = jnp.where(straight, pair, swap_half(pair))
            half = pl.ds(ROWS + (c // 2) * CELL, CELL)
            out[half, :] = jnp.where(low == (c % 2 == 0), x, out[half, :])

    walk(meta, info[25], total, visit, kept)


def finish(total, kept, info, meta, dkv, dq, back, earlier):
    n = len(earlier)
    shapes = [(OUT, 128), (OUT * (n + 1), 128), (OUT, 128), (OUT, 128)]
    return pl.pallas_call(
        functools.partial(finish_kernel, total, n, kept),
        out_shape=[jax.ShapeDtypeStruct(s, F32) for s in shapes],
        in_specs=[sspec()] * 2 + [vspec()] * (3 + n),
        out_specs=[vspec()] * 4,
        compiler_params=params(),
        cost_estimate=cost(1 << 10, 2 << 20),
        name="finish",
    )(info, meta, dkv, dq, back, *earlier)


def unpack_kernel(info, *refs):
    core, heads, (oq, ok, ov) = refs[0], refs[1:10], refs[10:]
    me = info[24]
    core_row = (OUT, 2 * OUT, 0)
    step = pl.program_id(0)

    def rows(s, h, row):
        if s == 1:
            return core[pl.ds(pl.multiple_of(core_row[h] + row, CELL), CELL), :]
        return heads[3 * h + (0, None, 1, 2)[s]][pl.ds(pl.multiple_of(row, CELL), CELL), :]

    def grads(s, c, h):
        return rows(s, h, (2 * step + c) * CELL)

    def query(s, c, h):
        x = rows(s, h, ROWS + step * CELL)
        return x, swap_half(x)

    for s in range(PLANE):
        j = lax.bitwise_xor(me, s)
        first = pl.ds(pl.multiple_of(j * 128, 128), 128)
        for c in range(2):
            r = pl.ds(c * CELL, CELL)
            a, b = grads(s, c, 0), grads(s, c, 1)
            ok[r, first] = join(a, swap_half(b))
            ov[r, first] = join(swap_half(a), b)
            x0, y0 = query(s, c, 0)
            x1, y1 = query(s, c, 1)
            oq[r, first] = join(x0, y1) if c % 2 == 0 else join(y0, x1)
    for s in (0, 2):
        j = lax.bitwise_xor(me, s)
        even = (j % 2) == 0
        last = pl.ds(pl.multiple_of((4 + j // 2) * 128, 128), 128)
        for c in range(2):
            r = pl.ds(c * CELL, CELL)
            u, w = grads(s, c, 2), grads(s + 1, c, 2)
            a, b = jnp.where(even, u, w), jnp.where(even, w, u)
            ok[r, last] = join(a, swap_half(b))
            ov[r, last] = join(swap_half(a), b)
            u, w = query(s, c, 2)[0], query(s + 1, c, 2)[0]
            a, b = jnp.where(even, u, w), jnp.where(even, w, u)
            oq[r, last] = join(a, swap_half(b)) if c % 2 == 0 else join(swap_half(a), b)


def unpack_heads(info, core, parts, features):
    return pl.pallas_call(
        unpack_kernel,
        out_shape=[jax.ShapeDtypeStruct((ROWS, features), F32)] * 3,
        grid=(2,),
        in_specs=[sspec()] + [vspec()] * 10,
        out_specs=[pl.BlockSpec((ROWS // 2, features), lambda i: (i, 0))] * 3,
        compiler_params=params(),
        cost_estimate=cost(1 << 20, 5 << 20),
        name="unpack_heads",
    )(info, core, *[x for part in parts for x in part])


def after(x, *earlier):
    return lax.optimization_barrier((x, *earlier))[0]


def along_z(x, step):
    count = lax.axis_size("ctx")
    return lax.ppermute(x, "ctx", [(i, (i + step * PLANE) % count) for i in range(count)])


def swap(x, bit):
    return lax.ppermute(x, "ctx", [(i, i ^ bit) for i in range(lax.axis_size("ctx"))])


def anywhere(flag):
    planes, groups = lax.axis_size("ctx") // PLANE, lax.axis_size("groups")
    if planes > HEADS + 1:
        flag = lax.pmax(flag, "ctx")
    for step in range(1, groups):
        route = [(i, (i + step) % groups) for i in range(groups)]
        flag = jnp.maximum(flag, lax.ppermute(flag, "groups", route))
    return flag


def gradients(kept, info, key_rows, value_rows, query_rows, grad_rows):
    total = lax.axis_size("ctx") * CELLS
    sizes = [6 * ROWS + 8] * 2 + [2 * ROWS + 8, 2 * ROWS, 2 * ROWS] * 2
    shapes = [(n, 128) for n in sizes]
    arrays = (key_rows, value_rows, query_rows, grad_rows)
    own, core, *rest = pack(pack_kernel, shapes, "pack_heads", info, *arrays)
    near, far = rest[:3], rest[3:]

    def across(h, *earlier):
        pair = (near[h], far[h])
        if earlier:
            pair = after(pair, *earlier)
        near[h], far[h] = swap(pair[0], 2), swap(pair[1], 3)

    across(0)
    core = swap(core, 1)
    across(1, core)
    first = (own, core, near[0], far[0])
    meta = jnp.stack([x[r, :32] for x, r in zip(first, META_ROWS)]).astype(jnp.int32)
    message = halo_message(total, 0, kept, info, meta, first, [])
    halo = [along_z(message, 1)]
    across(2, message)
    corner = (span(kept) + 2) * CELL
    meta_prev = halo[0][corner : corner + 4, :32].astype(jnp.int32)
    dkv, dq, back = [], [], []
    for h in range(HEADS):
        earlier = [*dq[-1:], message]
        if h < HEADS - 1:
            held = (own, core, near[h + 1], far[h + 1])
            info_h = after(info, *dq[-1:])
            message = halo_message(total, h + 1, kept, info_h, meta, held, halo)
            halo.append(along_z(message, 1))
            earlier.append(message)
        held = (own, core, near[h], far[h])
        outs = attend(total, h, kept, after(info, *earlier), meta, meta_prev, held, halo[h])
        dkv.append(outs[0])
        dq.append(outs[1])
        back.append(along_z(outs[2], -1))

    parts, cores = [], []

    def finish_head(h):
        earlier = cores[:] if h == HEADS - 1 else []
        info_h = after(info, *(dq[2:] if h < 2 else parts[0][1:] + parts[1][1:]))
        mine, core, near, far = finish(total, kept, info_h, meta, dkv[h], dq[h], back[h], earlier)
        cores.append(core)
        parts.append((mine, swap(near, 2), swap(far, 3)))

    for h in range(HEADS):
        finish_head(h)
    at = corner + PLANE
    flag = jnp.maximum(message[at : at + 1], halo[-1][at : at + 1]) if kept else None
    return flag, unpack_heads(info, swap(cores[-1], 1), parts, query_rows.shape[1])


def on_device(query_rows, key_rows, value_rows, grad_rows, placement, cell_lengths, gene_mask):
    count = lax.axis_size("ctx")
    total = count * CELLS
    index = lax.axis_index("ctx").astype(jnp.int32)
    plane = index // PLANE

    start = plane * (PLANE * CELLS)
    start_prev = lax.rem(start - PLANE * CELLS + total, total)
    tail = jnp.stack([jnp.int32(0)] * 4 + [index % PLANE, start, start_prev, jnp.int32(0)])
    info = jnp.concatenate([placement, cell_lengths, gene_mask.reshape(-1), tail])

    arrays = (key_rows, value_rows, query_rows, grad_rows)
    flag, outs = gradients(KEPT, info, *arrays)

    def again(carry):
        info = carry[1]
        _, outs = gradients(None, info, *arrays)
        return (jnp.bool_(False), info + 1, *outs)

    more = anywhere(flag)[0, 0] > 0.0
    return lax.while_loop(lambda carry: carry[0], again, (more, info, *outs))[2:]


def solution(mesh):
    rows = P(("groups", "ctx"), None)
    flat = P(("groups", "ctx"))
    return jax.shard_map(
        on_device,
        mesh=mesh,
        in_specs=(rows, rows, rows, rows, flat, flat, rows),
        out_specs=(rows, rows, rows),
        check_vma=False,
    )
```

```python
import functools

import jax
import jax.numpy as jnp
from jax import lax
from jax.experimental import pallas as pl
from jax.experimental.pallas import tpu as pltpu
from jax.sharding import PartitionSpec as P

HEAD_DIM = 64
CELL = 64
CELLS = 4
ROWS = 256
PLANE = 4
HEADS = 3
HALO = 14
ATTEND_COST = 1 << 26
BLOCK = 16
KEPT = 43
F32 = jnp.float32
BF16 = jnp.bfloat16
VMEM = pltpu.VMEM
NEGATIVE = -1e30
SCALE = HEAD_DIM ** -0.5


def vspec():
    return pl.BlockSpec(memory_space=pltpu.VMEM)


def sspec():
    return pl.BlockSpec(memory_space=pltpu.SMEM)


def params(limit=32):
    return pltpu.CompilerParams(vmem_limit_bytes=limit << 20)


def cost(flops, nbytes):
    return pl.CostEstimate(flops=flops, bytes_accessed=nbytes, transcendentals=0)


def lanes(shape):
    return lax.broadcasted_iota(jnp.int32, shape, 1)


def swap_half(x):
    return pltpu.roll(x, 64, 1)


def join(low, high):
    return jnp.where(lanes(low.shape) < 64, low, high)


def cells(i):
    return pl.ds(pl.multiple_of(i * CELL, CELL), CELL)


def head_blocks(info, c, s, a_ref, b_ref, grads):
    r = pl.ds(c * CELL, CELL)
    j = lax.bitwise_xor(info[24], s)
    first = pl.ds(pl.multiple_of(j * 128, 128), 128)
    last = pl.ds(pl.multiple_of((4 + j // 2) * 128, 128), 128)
    odd = (j % 2) == 1

    def load(lane_tile):
        a, b = a_ref[r, lane_tile], b_ref[r, lane_tile]
        if grads:
            row = lax.broadcasted_iota(jnp.int32, (CELL, 128), 0)
            a, b = a * SCALE, jnp.where(row < info[4 + c], b, 0.0)
        return a, b

    def zero():
        a, b = load(first)
        return join(a, swap_half(b))

    def one():
        a, b = load(first)
        return join(swap_half(a), b)

    def two():
        a, b = load(last)
        return join(jnp.where(odd, swap_half(a), a), jnp.where(odd, b, swap_half(b)))

    return zero, one, two


def pack_kernel(info, k_ref, v_ref, q_ref, g_ref, *outs):
    mine, near, far = outs[:2], outs[2:5], outs[5:8]
    lane = lax.broadcasted_iota(jnp.int32, (8, 128), 1)
    meta = jnp.zeros((8, 128), F32)
    for i in range(20):
        meta = jnp.where(lane == i, info[i].astype(F32), meta)
    for out, row0 in zip((*mine, near[0], far[0]), META_ROWS):
        out[pl.ds(row0, 8), :] = meta
    for s in (2, 3, 1, 0):
        for c in range(CELLS):
            kv = head_blocks(info, c, s, k_ref, v_ref, False)
            qg = head_blocks(info, c, s, q_ref, g_ref, True)
            for h in range(HEADS):
                if s < 2:
                    out, row0 = mine[s], 2 * ROWS * h
                else:
                    out, row0 = (near, far)[s - 2][h], 0
                out[pl.ds(row0 + c * CELL, CELL), :] = kv[h]()
                out[pl.ds(row0 + ROWS + c * CELL, CELL), :] = qg[h]()


PACKED = [(n, 128) for n in [6 * ROWS + 8] * 2 + [2 * ROWS + 8, 2 * ROWS, 2 * ROWS] * 2]
META_ROWS = (6 * ROWS, 6 * ROWS, 2 * ROWS, 2 * ROWS)


def pack(kernel, shapes, name, info, *arrays):
    return pl.pallas_call(
        kernel,
        out_shape=[jax.ShapeDtypeStruct(s, F32) for s in shapes],
        in_specs=[sspec()] + [vspec()] * len(arrays),
        out_specs=[vspec()] * len(shapes),
        compiler_params=params(),
        cost_estimate=cost(1 << 20, 3 << 20),
        name=name,
    )(info, *arrays)


def walk(meta, start, total, visit, kept=None):
    rank, count = jnp.int32(0), jnp.int32(0)
    for s in range(PLANE):
        for c in range(CELLS):
            rel = lax.rem(meta[s, c] - start + total, total)
            moved = rel >= 16
            slot = jnp.where(moved, 12 + rank, rel - 4)
            at = []
            for i in range(4 if kept else 0):
                seen = (rel >= 4) & (meta[s, 4 + c] > BLOCK * i)
                if i > 0:
                    seen = seen & (meta[s, 7 + 3 * c + i] == 0)
                at.append((seen, jnp.where(seen, jnp.minimum(count, kept), kept)))
                count = count + seen.astype(jnp.int32)
            visit(s, c, rel, slot, at)
            rank = rank + moved.astype(jnp.int32)
    return count


def span(kept):
    return (kept + 1) * BLOCK // CELL if kept else HALO


def block16(i):
    return pl.ds(pl.multiple_of(i * BLOCK, BLOCK), BLOCK)


def halo_kernel(total, h, kept, info, meta, *refs):
    parts, out = refs[:4], refs[-1]
    first = span(kept)
    if kept:
        out[block16(kept), :] = jnp.zeros((BLOCK, 128), F32)

    def visit(s, c, rel, slot, at):
        row0 = KV_ROWS[h][s] + c * CELL
        for i, (_, place) in enumerate(at):
            out[block16(place), :] = parts[s][pl.ds(row0 + BLOCK * i, BLOCK), :]
        if not kept:

            @pl.when(rel >= 4)
            def _():
                out[cells(slot), :] = parts[s][pl.ds(row0, CELL), :]

        @pl.when(rel >= 16)
        def _():
            out[cells(first + slot - 12), :] = parts[s][pl.ds(QG_ROWS[h][s] + c * CELL, CELL), :]

    count = walk(meta, info[25], total, visit, kept)
    if kept or h == 0:
        out[pl.ds((first + 2) * CELL, 8), :] = jnp.zeros((8, 128), F32)
        for s in range(PLANE if h == 0 else 0):
            out[pl.ds((first + 2) * CELL + s, 1), :] = parts[s][pl.ds(META_ROWS[s], 1), :]
    if kept:
        at = pl.ds((first + 2) * CELL + PLANE, 1)
        flag = jnp.full((1, 128), (count > kept).astype(F32))
        for came in refs[4:-1]:
            flag = jnp.maximum(flag, came[at, :])
        out[at, :] = flag


KV_ROWS = tuple((2 * h * ROWS, 2 * h * ROWS, 0, 0) for h in (0, 1, 2, 0))
LAST = HEADS
QG_ROWS = tuple(tuple(r + ROWS for r in rows) for rows in KV_ROWS)


def halo_message(total, h, kept, info, meta, parts, came):
    came = came[-1:] if kept else []
    rows = (span(kept) + 2) * CELL + (8 if kept or h == 0 else 0)
    return pl.pallas_call(
        functools.partial(halo_kernel, total, h, kept),
        out_shape=jax.ShapeDtypeStruct((rows, 128), F32),
        in_specs=[sspec()] * 2 + [vspec()] * (4 + len(came)),
        out_specs=vspec(),
        compiler_params=params(),
        cost_estimate=cost(1 << 10, 1 << 20),
        name="halo_message",
    )(info, meta, *parts, *came)


def split(x):
    high = x.astype(BF16).astype(F32)
    return high, x - high


def nt(a, b):
    return lax.dot_general(a, b, (((1,), (1,)), ((), ())), preferred_element_type=F32)


def nn(a, b):
    return lax.dot_general(a, b, (((1,), (0,)), ((), ())), preferred_element_type=F32)


def tn(a, b):
    return lax.dot_general(a, b, (((0,), (0,)), ((), ())), preferred_element_type=F32)


def attend_kernel(total, h, kept, info, meta, meta_prev, *refs):
    here_parts, halo = refs[:4], refs[4]
    dkv, dq, back = refs[5:8]
    kcat, vcat, kt, acc_k, acc_v, qcat, gcat, qrhs, grhs, dq_scr = refs[8:18]
    pairs = (refs[18:20], refs[20:22])
    start = info[25]
    start_prev = info[26]
    lane = lax.broadcasted_iota(jnp.int32, (CELL, 128), 1)
    low = lane < 64
    lane16 = lax.broadcasted_iota(jnp.int32, (16, 128), 1)
    row16 = lax.broadcasted_iota(jnp.int32, (16, 128), 0)

    def put_key(x, slot, m, s, c):
        length = m[s, 4 + c]
        parts = []
        for i in range(4):
            limit = length - 16 * i
            if i > 0:
                limit = jnp.where(m[s, 7 + 3 * c + i] > 0, 0, limit)
            parts.append(jnp.where((row16 >= limit) & (lane16 == 64), NEGATIVE, 0.0))
        bias = jnp.concatenate(parts, axis=0)
        high, rest = split(x)
        high_r, rest_r = swap_half(high), swap_half(rest)
        mid, least = split(rest)
        kcat[cells(slot), pl.ds(0, 128)] = jnp.where(low, high, rest_r).astype(BF16)
        kcat[cells(slot), pl.ds(128, 128)] = jnp.where(low, high, bias).astype(BF16)
        kcat[cells(slot), pl.ds(256, 128)] = jnp.where(low, mid, swap_half(least)).astype(BF16)
        kcat[cells(slot), pl.ds(384, 128)] = jnp.where(low, high, 0.0).astype(BF16)
        vcat[cells(slot), pl.ds(0, 128)] = jnp.where(low, high_r, rest).astype(BF16)
        vcat[cells(slot), pl.ds(128, 128)] = jnp.where(low, high_r, 0.0).astype(BF16)

    one = jnp.where(lane == 64, 1.0, 0.0)

    def put_query(x, slot):
        high, rest = split(x)
        high_r, rest_r = swap_half(high), swap_half(rest)
        qcat[cells(slot), pl.ds(0, 128)] = jnp.where(low, high, high_r).astype(BF16)
        qcat[cells(slot), pl.ds(128, 128)] = jnp.where(low, rest, one).astype(BF16)
        mid, least = split(rest)
        qcat[cells(slot), pl.ds(256, 128)] = jnp.where(low, mid, high_r).astype(BF16)
        qcat[cells(slot), pl.ds(384, 128)] = jnp.where(low, least, 0.0).astype(BF16)
        gcat[cells(slot), pl.ds(0, 128)] = jnp.where(low, high_r, high).astype(BF16)
        gcat[cells(slot), pl.ds(128, 128)] = jnp.where(low, rest_r, 0.0).astype(BF16)
        qrhs[cells(slot), :] = jnp.where(low, high, rest_r).astype(BF16)
        grhs[cells(slot), :] = jnp.where(low, rest_r, high).astype(BF16)

    def own(s, c, rel, slot, at):
        here = rel < 16
        put_key(here_parts[s][pl.ds(KV_ROWS[h][s] + c * CELL, CELL), :], jnp.where(here, 12 + rel, 28), meta, s, c)
        put_query(here_parts[s][pl.ds(QG_ROWS[h][s] + c * CELL, CELL), :], jnp.where(here, rel, 16))

    walk(meta, start, total, own)
    came = [jnp.int32(0), jnp.int32(0)]

    def before(s, c, rel, slot, at):
        here = rel >= 4
        if kept:
            x = jnp.concatenate([halo[block16(place), :] for _, place in at], axis=0)
        else:
            x = halo[cells(jnp.where(here, slot, 0)), :]
        put_key(x, jnp.where(here, rel - 4, 28), meta_prev, s, c)
        for i in range(2):
            came[i] = jnp.where((rel >= 16) & (slot == 12 + i), rel - 16, came[i])

    walk(meta_prev, start_prev, total, before, kept)
    for i in range(2):
        put_query(halo[pl.ds((span(kept) + i) * CELL, CELL), :], came[i])
    for j in range(7):
        kt[:, pl.ds(j * ROWS, ROWS)] = kcat[pl.ds(j * ROWS, ROWS), pl.ds(0, 128)].T
    acc_k[...] = jnp.zeros(acc_k.shape, F32)
    acc_v[...] = jnp.zeros(acc_v.shape, F32)

    def fold(x, op):
        out = x[0:8]
        for i in range(1, x.shape[0] // 8):
            out = op(out, x[8 * i : 8 * i + 8])
        return out

    def block(b, carry, side=0):
        s_scr, d_scr = pairs[side]

        def rows(i, n=ROWS):
            return pl.ds(i * ROWS if isinstance(i, int) else pl.multiple_of(i * ROWS, ROWS), n)

        q_rows = rows(b)
        top = None
        for c in range(4):
            scores = nt(kcat[rows(b + c), :], qcat[q_rows, :])
            s_scr[rows(c), :] = scores
            part = fold(scores, jnp.maximum)
            top = part if top is None else jnp.maximum(top, part)
        top = jnp.max(top, axis=0, keepdims=True)
        size = jnp.zeros((8, ROWS), F32)
        dots = jnp.zeros((8, ROWS), F32)
        for c in range(4):
            weights = jnp.exp(s_scr[rows(c), :] - top)
            grad_weights = nt(vcat[rows(b + c), :], gcat[q_rows, :])
            d_scr[rows(c), :] = grad_weights
            s_scr[rows(c), :] = weights
            size = size + fold(weights, jnp.add)
            dots = dots + fold(weights * grad_weights, jnp.add)
        inverse = 1.0 / jnp.sum(size, axis=0, keepdims=True)
        delta = jnp.sum(dots, axis=0, keepdims=True) * inverse
        dq_t = jnp.zeros((128, ROWS), F32)
        for c in range(4):
            weights = s_scr[rows(c), :] * inverse
            grad_scores = weights * (d_scr[rows(c), :] - delta)
            high = weights.astype(BF16)
            rest = (weights - high.astype(F32)).astype(BF16)
            acc_v[rows(b + c), :] += nn(high, grhs[q_rows, :]) + nn(rest, grhs[q_rows, :])
            high = grad_scores.astype(BF16)
            rest = (grad_scores - high.astype(F32)).astype(BF16)
            acc_k[rows(b + c), :] += nn(high, qrhs[q_rows, :]) + nn(rest, qrhs[q_rows, :])
            keys = kt[:, rows(b + c)]
            dq_t = dq_t + nn(keys, high) + nn(keys, rest)
        dq_t = (dq_t[0:64] + dq_t[64:128]) * SCALE
        dq_scr[q_rows, :] = jnp.concatenate([dq_t, dq_t], axis=0).T
        return carry

    if kept:
        lax.fori_loop(0, 2, lambda i, _: block(2 * i + 1, block(2 * i, 0, 0), 1), 0)
    else:
        lax.fori_loop(0, 4, block, 0)

    def grad_kv(slot):
        a = acc_k[cells(slot), :]
        b = acc_v[cells(slot), :]
        return jnp.where(low, a + swap_half(a), b + swap_half(b))

    def own_out(s, c, rel, slot, at):
        here = rel < 16
        x = grad_kv(jnp.where(here, 12 + rel, 0))
        dkv[pl.ds(s * ROWS + c * CELL, CELL), :] = jnp.where(here, x, 0.0)
        x = dq_scr[cells(jnp.where(here, rel, 0)), :]
        half = pl.ds(s * 128 + (c // 2) * CELL, CELL)
        if c % 2 == 0:
            dq[half, :] = x
        else:
            dq[half, :] = jnp.where(low, dq[half, :], x)

    walk(meta, start, total, own_out)

    def before_out(s, c, rel, slot, at):
        here = rel >= 4
        x = grad_kv(jnp.where(here, rel - 4, 0))
        for i, (_, place) in enumerate(at):
            back[block16(place), :] = x[BLOCK * i : BLOCK * (i + 1)]
        if not kept:
            back[cells(jnp.where(here, slot, HALO)), :] = x

    walk(meta_prev, start_prev, total, before_out, kept)
    pair = jnp.where(low, dq_scr[cells(came[0]), :], dq_scr[cells(came[1]), :])
    back[pl.ds(span(kept) * CELL, CELL), :] = pair


def attend(total, h, kept, info, meta, meta_prev, parts, halo):
    shapes = [(4 * ROWS, 128), (2 * ROWS, 128), ((span(kept) + 1) * CELL, 128)]
    keys, queries = 29 * CELL, 17 * CELL
    return pl.pallas_call(
        functools.partial(attend_kernel, total, h, kept),
        out_shape=[jax.ShapeDtypeStruct(s, F32) for s in shapes],
        in_specs=[sspec()] * 3 + [vspec()] * 5,
        out_specs=[vspec()] * 3,
        scratch_shapes=[
            VMEM((keys, 512), BF16),
            VMEM((keys, 256), BF16),
            VMEM((128, 28 * CELL), BF16),
            VMEM((28 * CELL, 128), F32),
            VMEM((28 * CELL, 128), F32),
            VMEM((queries, 512), BF16),
            VMEM((queries, 256), BF16),
            VMEM((queries, 128), BF16),
            VMEM((queries, 128), BF16),
            VMEM((queries, 128), F32),
        ]
        + [VMEM((4 * ROWS, ROWS), F32)] * 4,
        compiler_params=params(24),
        cost_estimate=cost(ATTEND_COST, 1 << 20),
        name="attend",
    )(info, meta, meta_prev, *parts, halo)


OUT = ROWS + ROWS // 2


def finish_kernel(total, n, kept, info, meta, dkv, dq, back, *refs):
    earlier, outs = refs[:n], refs[n:]
    for i in range(n):
        outs[1][pl.ds((i + 1) * OUT, OUT), :] = earlier[i][...]
    low = lanes((CELL, 128)) < 64
    pair = back[pl.ds(span(kept) * CELL, CELL), :]
    for s in range(PLANE):
        outs[s][pl.ds(ROWS, 128), :] = dq[pl.ds(s * 128, 128), :]

    def visit(s, c, rel, slot, at):
        out = outs[s]
        sent = rel >= 4
        if kept:
            x = [jnp.where(seen, back[block16(place), :], 0.0) for seen, place in at]
            x = jnp.concatenate(x, axis=0)
        else:
            x = jnp.where(sent, back[cells(jnp.where(sent, slot, 0)), :], 0.0)
        out[pl.ds(c * CELL, CELL), :] = dkv[pl.ds(s * ROWS + c * CELL, CELL), :] + x

        @pl.when(rel >= 16)
        def _():
            straight = (slot - 12) == (c % 2)
            x = jnp.where(straight, pair, swap_half(pair))
            half = pl.ds(ROWS + (c // 2) * CELL, CELL)
            out[half, :] = jnp.where(low == (c % 2 == 0), x, out[half, :])

    walk(meta, info[25], total, visit, kept)


def finish(total, kept, info, meta, dkv, dq, back, earlier):
    n = len(earlier)
    shapes = [(OUT, 128), (OUT * (n + 1), 128), (OUT, 128), (OUT, 128)]
    return pl.pallas_call(
        functools.partial(finish_kernel, total, n, kept),
        out_shape=[jax.ShapeDtypeStruct(s, F32) for s in shapes],
        in_specs=[sspec()] * 2 + [vspec()] * (3 + n),
        out_specs=[vspec()] * 4,
        compiler_params=params(),
        cost_estimate=cost(1 << 10, 2 << 20),
        name="finish",
    )(info, meta, dkv, dq, back, *earlier)


def unpack_kernel(info, *refs):
    core, heads, (oq, ok, ov) = refs[0], refs[1:10], refs[10:]
    me = info[24]
    core_row = (OUT, 2 * OUT, 0)
    step = pl.program_id(0)

    def rows(s, h, row):
        if s == 1:
            return core[pl.ds(pl.multiple_of(core_row[h] + row, CELL), CELL), :]
        return heads[3 * h + (0, None, 1, 2)[s]][pl.ds(pl.multiple_of(row, CELL), CELL), :]

    def grads(s, c, h):
        return rows(s, h, (2 * step + c) * CELL)

    def query(s, c, h):
        x = rows(s, h, ROWS + step * CELL)
        return x, swap_half(x)

    for s in range(PLANE):
        j = lax.bitwise_xor(me, s)
        first = pl.ds(pl.multiple_of(j * 128, 128), 128)
        for c in range(2):
            r = pl.ds(c * CELL, CELL)
            a, b = grads(s, c, 0), grads(s, c, 1)
            ok[r, first] = join(a, swap_half(b))
            ov[r, first] = join(swap_half(a), b)
            x0, y0 = query(s, c, 0)
            x1, y1 = query(s, c, 1)
            oq[r, first] = join(x0, y1) if c % 2 == 0 else join(y0, x1)
    for s in (0, 2):
        j = lax.bitwise_xor(me, s)
        even = (j % 2) == 0
        last = pl.ds(pl.multiple_of((4 + j // 2) * 128, 128), 128)
        for c in range(2):
            r = pl.ds(c * CELL, CELL)
            u, w = grads(s, c, 2), grads(s + 1, c, 2)
            a, b = jnp.where(even, u, w), jnp.where(even, w, u)
            ok[r, last] = join(a, swap_half(b))
            ov[r, last] = join(swap_half(a), b)
            u, w = query(s, c, 2)[0], query(s + 1, c, 2)[0]
            a, b = jnp.where(even, u, w), jnp.where(even, w, u)
            oq[r, last] = join(a, swap_half(b)) if c % 2 == 0 else join(swap_half(a), b)


def unpack_heads(info, core, parts, features):
    return pl.pallas_call(
        unpack_kernel,
        out_shape=[jax.ShapeDtypeStruct((ROWS, features), F32)] * 3,
        grid=(2,),
        in_specs=[sspec()] + [vspec()] * 10,
        out_specs=[pl.BlockSpec((ROWS // 2, features), lambda i: (i, 0))] * 3,
        compiler_params=params(),
        cost_estimate=cost(1 << 20, 5 << 20),
        name="unpack_heads",
    )(info, core, *[x for part in parts for x in part])


def after(x, *earlier):
    return lax.optimization_barrier((x, *earlier))[0]


def along_z(x, step):
    count = lax.axis_size("ctx")
    return lax.ppermute(x, "ctx", [(i, (i + step * PLANE) % count) for i in range(count)])


def swap(x, bit):
    return lax.ppermute(x, "ctx", [(i, i ^ bit) for i in range(lax.axis_size("ctx"))])


def anywhere(flag):
    planes, groups = lax.axis_size("ctx") // PLANE, lax.axis_size("groups")
    if planes > HEADS + 1:
        flag = lax.pmax(flag, "ctx")
    for step in range(1, groups):
        route = [(i, (i + step) % groups) for i in range(groups)]
        flag = jnp.maximum(flag, lax.ppermute(flag, "groups", route))
    return flag


def gradients(kept, info, key_rows, value_rows, query_rows, grad_rows):
    total = lax.axis_size("ctx") * CELLS
    arrays = (key_rows, value_rows, query_rows, grad_rows)
    own, core, *rest = pack(pack_kernel, PACKED, "pack_heads", info, *arrays)
    near, far = rest[:3], rest[3:]

    def across(h, *earlier):
        pair = (near[h], far[h])
        if earlier:
            pair = after(pair, *earlier)
        near[h], far[h] = swap(pair[0], 2), swap(pair[1], 3)

    across(0)
    core = swap(core, 1)
    across(1, core)
    first = (own, core, near[0], far[0])
    meta = jnp.stack([x[r, :32] for x, r in zip(first, META_ROWS)]).astype(jnp.int32)
    message = halo_message(total, 0, kept, info, meta, first, [])
    halo = [along_z(message, 1)]
    across(2, message)
    corner = (span(kept) + 2) * CELL
    meta_prev = halo[0][corner : corner + 4, :32].astype(jnp.int32)
    dkv, dq, back = [], [], []
    for h in range(HEADS):
        earlier = [*dq[-1:], message]
        if h < HEADS - 1:
            held = (own, core, near[h + 1], far[h + 1])
            info_h = after(info, *dq[-1:])
            message = halo_message(total, h + 1, kept, info_h, meta, held, halo)
            halo.append(along_z(message, 1))
            earlier.append(message)
        held = (own, core, near[h], far[h])
        outs = attend(total, h, kept, after(info, *earlier), meta, meta_prev, held, halo[h])
        dkv.append(outs[0])
        dq.append(outs[1])
        back.append(along_z(outs[2], -1))

    parts, cores = [], []

    def finish_head(h):
        earlier = cores[:] if h == HEADS - 1 else []
        info_h = after(info, *(dq[2:] if h < 2 else parts[0][1:] + parts[1][1:]))
        mine, core, near, far = finish(total, kept, info_h, meta, dkv[h], dq[h], back[h], earlier)
        cores.append(core)
        parts.append((mine, swap(near, 2), swap(far, 3)))

    for h in range(HEADS):
        finish_head(h)
    at = corner + PLANE
    flag = jnp.maximum(message[at : at + 1], halo[-1][at : at + 1]) if kept else None
    return flag, unpack_heads(info, swap(cores[-1], 1), parts, query_rows.shape[1])


def dense_gradients(info, *arrays):
    total = lax.axis_size("ctx") * CELLS
    own, core, *rest = pack(pack_kernel, PACKED, "pack_heads", info, *arrays)
    core = swap(core, 1)
    near, far = [swap(x, 2) for x in rest[:3]], [swap(x, 3) for x in rest[3:]]
    first = (own, core, near[0], far[0])
    corner = jnp.concatenate([x[r : r + 1] for x, r in zip(first, META_ROWS)])
    meta = corner[:, :32].astype(jnp.int32)
    meta_prev = along_z(jnp.concatenate([corner, corner]), 1)[:4, :32].astype(jnp.int32)
    rows = 2 * ROWS
    mine = [x[: HEADS * rows].reshape(HEADS, rows, 128) for x in (own, core)]
    theirs = [jnp.stack([x[:rows] for x in part]) for part in (near, far)]

    def head(carry, parts):
        message = halo_message(total, LAST, None, info, meta, parts, [])
        dkv, dq, back = attend(
            total, LAST, None, info, meta, meta_prev, parts, along_z(message, 1)
        )
        outs = finish(total, None, info, meta, dkv, dq, along_z(back, -1), [])
        return carry, (outs[0], *[swap(x, i + 1) for i, x in enumerate(outs[1:])])

    _, outs = lax.scan(head, jnp.int32(0), (*mine, *theirs))
    core = jnp.concatenate([outs[1][2], outs[1][0], outs[1][1]])
    parts = [(outs[0][h], outs[2][h], outs[3][h]) for h in range(HEADS)]
    return unpack_heads(info, core, parts, arrays[0].shape[1])


def on_device(query_rows, key_rows, value_rows, grad_rows, placement, cell_lengths, gene_mask):
    count = lax.axis_size("ctx")
    total = count * CELLS
    index = lax.axis_index("ctx").astype(jnp.int32)
    plane = index // PLANE

    start = plane * (PLANE * CELLS)
    start_prev = lax.rem(start - PLANE * CELLS + total, total)
    tail = jnp.stack([jnp.int32(0)] * 4 + [index % PLANE, start, start_prev, jnp.int32(0)])
    info = jnp.concatenate([placement, cell_lengths, gene_mask.reshape(-1), tail])

    arrays = (key_rows, value_rows, query_rows, grad_rows)
    flag, outs = gradients(KEPT, info, *arrays)

    def again(carry):
        info = carry[1]
        outs = dense_gradients(info, *arrays)
        return (jnp.bool_(False), info + 1, *outs)

    more = anywhere(flag)[0, 0] > 0.0
    return lax.while_loop(lambda carry: carry[0], again, (more, info, *outs))[2:]


def solution(mesh):
    rows = P(("groups", "ctx"), None)
    flat = P(("groups", "ctx"))
    return jax.shard_map(
        on_device,
        mesh=mesh,
        in_specs=(rows, rows, rows, rows, flat, flat, rows),
        out_specs=(rows, rows, rows),
        check_vma=False,
    )
```
